256 devices in a mesh: scan: 4 (over y), slab: 64 (over z, x, core).
Axes of the slice: x: 4, y: 4, z: 8, core: 2. Of those that a mesh axis runs over, the one named last changes fastest.
Arguments:
- volume: float32 [4, 32768, 1024], P('scan', 'slab'), may hold values from -108 to 108
- velocity0: float32 [4, 32768], P('scan', 'slab'), may hold values from -0.5 to 0.5
- fetch_slab: int32 [4, 2, 32768, 1], P('scan', None, 'slab'), may hold values from 0 to 63; in each aligned block of 512 rows (0 to 511, 512 to 1023, ..., all dimensions but the last counted through in order) at most 12 rows name the same one
- fetch_row: int32 [4, 2, 32768], P('scan', None, 'slab'), may hold values from 0 to 511
- modulus_class: int32 [4, 32768], P('scan', 'slab'), may hold values from 0 to 3
- modulus_table: float32 [4], replicated, may hold values from 200 to 3000
Outputs:
- velocity: float32 [4, 32768], P('scan', 'slab')
- misfit: float32 [4, 32768, 1024], P('scan', 'slab')
The draws below stay inside these ranges and needn't reach their ends.
Inputs may be any that keep to these rules, and one draw needn't show every extreme that they name: `fetch_slab`: among the rows of one device for one direction, at most 12 name the same slab, a bound that some block reaches of them.
All inputs are finite; a program needn't handle non-finite values.
Results may differ from the reference program's by a relative error of at most 0.00011.
Values sent between devices are 32-bit elements; how exact they have to be, the bound alone decides.
A program may use at most 64 MiB of HBM per device.

```python
import math
import jax
import jax.numpy as jnp
import numpy as np
from jax import lax

X = 1024
RD = 512
Y = 1024
BAND = 32
NCLASS = 4
ITERS = 2
SCANS = 4
ROWS = 32768
CAP = 12
N_SLAB = 64


def draw_volume(key, part):
    keys = jax.random.split(key, 3)
    shape = (SCANS, ROWS, X)
    base = jnp.clip(jax.random.normal(keys[0], shape, jnp.float32), -6.0, 6.0)
    contrast = jnp.exp(jax.random.uniform(keys[1], (SCANS, ROWS, 1), jnp.float32, math.log(0.3), math.log(3.0)))
    columns = jnp.exp(jax.random.uniform(keys[2], (1, 1, X), jnp.float32, math.log(0.5), math.log(2.0)))
    position = lax.broadcasted_iota(jnp.int32, (1, ROWS, 1), 1).astype(jnp.float32)
    ramp = 1.0 + 2.0 * position / float(max(ROWS - 1, 1))
    return base * contrast * columns * ramp


def set_ends(entries, own_key, least, top_value):
    index_at = [jax.random.randint(jax.random.fold_in(own_key, axis), (), 0, length) for axis, length in enumerate(entries.shape)]
    longest = entries.shape.index(max(entries.shape))
    neighbour = index_at[:longest] + [(index_at[longest] + 1) % entries.shape[longest]] + index_at[longest + 1:]
    return entries.at[tuple(index_at)].set(least).at[tuple(neighbour)].set(top_value)


def level_of(key, shape, cuts, low, high):
    gain = 1.0
    for axis_at, parts in cuts:
        heights = jax.random.uniform(jax.random.fold_in(jax.random.fold_in(key, 6), axis_at), (parts,), jnp.float32, low / len(cuts), high / len(cuts))
        gain = gain * jnp.repeat(jnp.exp(heights), shape[axis_at] // parts).reshape((-1,) + (1,) * (len(shape) - 1 - axis_at))
    return gain


def routed_block(own_key, own, number, rows, amount, top, bound, skew):
    ranking = jax.random.permutation(own_key, amount)
    packed, ordinary = portions_of(amount, rows * top, bound, skew, True), portions_of(amount, rows * top, bound, skew, False)
    places = jnp.arange(amount)

    def named(sizes, rotation):
        used = int((sizes > 0).sum())
        fixed = max(1, used // 4)
        passed = fixed + (places - fixed + rotation * (used - fixed)) % max(1, amount - fixed)
        return jnp.zeros((amount,), jnp.int32).at[ranking[jnp.where(places < fixed, places, passed)]].set(jnp.asarray(sizes, jnp.int32))

    sizes = jnp.where(number % 4 == 0, named(packed, number // 4), named(ordinary, number - number // 4 - 1))
    mixed = jax.random.permutation(jax.random.fold_in(own, 3), amount)
    source_of, sink = mixed[0:amount // 2 * 2:2], mixed[1:amount // 2 * 2:2]
    room = jnp.minimum(sizes[source_of] - 1, bound - sizes[sink]) // 2
    room = jnp.where((source_of == ranking[0]) | (sink == ranking[0]) | (sizes[sink] == 0), 0, jnp.maximum(room, 0))
    passed = jax.random.randint(jax.random.fold_in(own, 4), (amount // 2,), 0, 1 << 20) % (room + 1)
    sizes = sizes.at[source_of].add(-passed).at[sink].add(passed)
    labels = jnp.searchsorted(jnp.cumsum(sizes), jnp.arange(rows * top), side="right").astype(jnp.int32)
    table = labels.reshape(top, rows).T
    table = table[jax.random.permutation(jax.random.fold_in(own, 1), rows)]
    rotation = jax.random.randint(jax.random.fold_in(own, 2), (rows, 1), 0, top)
    return jnp.take_along_axis(table, (jnp.arange(top)[None, :] + rotation) % top, axis=1)


def portions_of(number_of, total, limit, lean, full):
    weights = [(1 << 20) // math.isqrt(grade ** lean) + 1 for grade in range(1, number_of + 1)]
    largest = limit if full else min(limit, max(-(-total // number_of), total * weights[0] // sum(weights)))
    least = 1 if total - largest >= number_of - 1 else 0
    holding, rest = [largest] + [least] * (number_of - 1), total - largest - least * (number_of - 1)
    while rest > 0:
        candidates = [i for i in range(1, number_of) if holding[i] < largest] or [i for i in range(1, number_of) if holding[i] < limit]
        mass, budget = sum([weights[i] for i in candidates]), rest
        for i in candidates:
            more = min(limit - holding[i], max(1, budget * weights[i] // mass), rest)
            holding[i] = holding[i] + more
            rest = rest - more
    return np.array(holding)


def setup_inputs(seed: int = 0) -> dict:
    key_list = jax.random.split(jax.random.key(seed), 7)
    volume = draw_volume(jax.random.fold_in(key_list[6], 71), 0)
    velocity0 = jnp.clip(jax.random.uniform(key_list[1], (SCANS, ROWS), jnp.float32, -0.5, 0.5) * level_of(key_list[1], (SCANS, ROWS), ((0, 4), (1, 64)), -0.4, 0.0), -0.5, 0.5)
    fetch_slab_keys = jax.random.split(jax.random.fold_in(key_list[2], 1), SCANS * 2 * ROWS // RD)
    fetch_slab_turns = jax.random.permutation(jax.random.fold_in(key_list[2], 3), SCANS * 2 * ROWS // RD)
    fetch_slab = jax.vmap(lambda own, number: routed_block(jax.random.fold_in(key_list[2], 2), own, number, RD, N_SLAB, 1, CAP, 2))(fetch_slab_keys, fetch_slab_turns).reshape((SCANS, 2, ROWS, 1))
    fetch_row = set_ends(jax.random.randint(key_list[3], (SCANS, 2, ROWS), 0, RD), jax.random.fold_in(key_list[3], 1), 0, RD - 1).astype(jnp.int32)
    modulus_class = set_ends(jax.random.randint(key_list[4], (SCANS, ROWS), 0, NCLASS), jax.random.fold_in(key_list[4], 1), 0, NCLASS - 1).astype(jnp.int32)
    modulus_table = jnp.clip(jnp.exp(jax.random.uniform(key_list[5], (NCLASS,), jnp.float32, math.log(200.0), math.log(3000.0))), 200.0, 3000.0)
    return {"volume": volume, "velocity0": velocity0, "fetch_slab": fetch_slab, "fetch_row": fetch_row, "modulus_class": modulus_class, "modulus_table": modulus_table}


root_three = math.sqrt(3.0)
pole_value = math.sqrt(3.0) - 2.0

def filter_block(block_width, band_reach):
    offsets = lax.broadcasted_iota(jnp.int32, (3 * block_width, block_width), 0) - block_width - lax.broadcasted_iota(jnp.int32, (3 * block_width, block_width), 1)
    distance = jnp.abs(offsets)
    parity = 1.0 - 2.0 * (distance % 2).astype(jnp.float32)
    magnitude = jnp.exp(distance.astype(jnp.float32) * math.log(-pole_value))
    return jnp.where(distance <= band_reach, root_three * parity * magnitude, jnp.zeros_like(magnitude))

def prefilter(voxels):
    length = voxels.shape[1]
    block_width = min(128, length)
    matrix = filter_block(block_width, BAND)
    padded = jnp.pad(voxels, ((0, 0), (block_width, block_width)))
    pieces = []
    for number in range(length // block_width):
        window = padded[:, number * block_width:number * block_width + 3 * block_width]
        pieces.append(jnp.dot(window, matrix, preferred_element_type=jnp.float32, precision=lax.Precision.HIGHEST))
    return jnp.concatenate(pieces, axis=1)

def taylor_terms(coeffs):
    padded = jnp.pad(coeffs, ((0, 0), (1, 1)))
    before = padded[:, :-2]
    after = padded[:, 2:]
    value = (before + 4.0 * coeffs + after) / 6.0
    slope = 0.5 * (after - before)
    bend = after - 2.0 * coeffs + before
    return (value, slope, bend)

def residuals(forward, backward, voxels, velocity):
    moved = velocity[:, None]
    fwd_value, fwd_slope, fwd_bend = taylor_terms(forward)
    bwd_value, bwd_slope, bwd_bend = taylor_terms(backward)
    res_fwd = fwd_value + moved * fwd_slope + 0.5 * moved * moved * fwd_bend - voxels
    jac_fwd = fwd_slope + moved * fwd_bend
    res_bwd = bwd_value - moved * bwd_slope + 0.5 * moved * moved * bwd_bend - voxels
    jac_bwd = moved * bwd_bend - bwd_slope
    return (res_fwd, jac_fwd, res_bwd, jac_bwd)

def row_terms(forward, backward, voxels, velocity):
    res_fwd, jac_fwd, res_bwd, jac_bwd = residuals(forward, backward, voxels, velocity)
    linear = lax.optimization_barrier(jnp.sum(jac_fwd * res_fwd + jac_bwd * res_bwd, axis=1))
    curvature = lax.optimization_barrier(jnp.sum(jac_fwd * jac_fwd + jac_bwd * jac_bwd, axis=1))
    return (linear, curvature)

def laplace(extended, margin, reach, length):
    centre = lax.slice_in_dim(extended, margin, margin + length)
    near = lax.slice_in_dim(extended, margin - 1, margin - 1 + length) + lax.slice_in_dim(extended, margin + 1, margin + 1 + length)
    far = lax.slice_in_dim(extended, margin - reach, margin - reach + length) + lax.slice_in_dim(extended, margin + reach, margin + reach + length)
    return 4.0 * centre - near - far

def stencil(field):
    length = field.shape[0]
    return laplace(jnp.pad(field, (Y, Y)), Y, Y, length)

def reference(volume, velocity0, fetch_slab, fetch_row, modulus_class, modulus_table):
    scans = volume.shape[0]
    coefficients = [prefilter(volume[number]) for number in range(scans)]
    forwards = []
    backwards = []
    for number in range(scans):
        index_fwd = (fetch_slab[number, 0, :, 0] * RD + fetch_row[number, 0]).astype(jnp.int32)
        index_bwd = (fetch_slab[number, 1, :, 0] * RD + fetch_row[number, 1]).astype(jnp.int32)
        if number + 1 < scans:
            forwards.append(jnp.take(coefficients[number + 1], index_fwd, axis=0))
        else:
            forwards.append(jnp.zeros_like(volume[number]))
        if number > 0:
            backwards.append(jnp.take(coefficients[number - 1], index_bwd, axis=0))
        else:
            backwards.append(jnp.zeros_like(volume[number]))
    coefficients = None
    classes = lax.broadcasted_iota(jnp.int32, (1, 1, modulus_table.shape[0]), 2)
    weight = lax.optimization_barrier(jnp.sum(jnp.where(modulus_class[:, :, None] == classes, modulus_table[None, None, :], jnp.zeros_like(modulus_table)[None, None, :]), axis=2))
    stiffness = jnp.sqrt(weight)
    velocity = velocity0
    for iteration in range(ITERS):
        linears = []
        curvatures = []
        for number in range(scans):
            linear, curvature = row_terms(forwards[number], backwards[number], volume[number], velocity[number])
            linears.append(linear)
            curvatures.append(curvature)
        linear = jnp.stack(linears)
        curvature = jnp.stack(curvatures)
        scaled = stiffness * velocity
        gradient = linear + stiffness * jnp.stack([stencil(scaled[number]) for number in range(scans)])
        diagonal = curvature + 4.0 * stiffness * stiffness
        direction = gradient / diagonal
        scaled_dir = stiffness * direction
        bend_term = scaled_dir * jnp.stack([stencil(scaled_dir[number]) for number in range(scans)])
        upper = jnp.sum(direction * gradient)
        lower = jnp.sum(curvature * direction * direction + bend_term)
        velocity = velocity - upper / lower * direction
    misfits = []
    for number in range(scans):
        res_fwd, jac_fwd, res_bwd, jac_bwd = residuals(forwards[number], backwards[number], volume[number], velocity[number])
        misfits.append(res_fwd + res_bwd)
    return (velocity, jnp.stack(misfits))
```

```python
import math

import jax
import jax.numpy as jnp
import numpy as np
from jax import lax
from jax.experimental import pallas as pl
from jax.experimental.pallas import tpu as pltpu
from jax.sharding import PartitionSpec as P

BAND = 32
ITERS = 2
CAP = 12
LANES = 128
MESH = pl.DeviceIdType.MESH

root_three = math.sqrt(3.0)
pole_value = math.sqrt(3.0) - 2.0


def slots_kernel(peer_ref, row_ref, request_ref, place_ref):
    slabs = request_ref.shape[1]
    rows = peer_ref.shape[1]
    earlier = (
        lax.broadcasted_iota(jnp.int32, (rows, rows), 0)
        < lax.broadcasted_iota(jnp.int32, (rows, rows), 1)
    ).astype(jnp.float32).astype(jnp.bfloat16)
    for side in range(2):
        peer = peer_ref[side : side + 1, :]
        row = row_ref[side : side + 1, :]
        named = (lax.broadcasted_iota(jnp.int32, (slabs, rows), 0) == peer).astype(jnp.float32)
        named16 = named.astype(jnp.bfloat16)
        before = jnp.dot(named16, earlier, preferred_element_type=jnp.float32)
        slot = jnp.sum(before * named, axis=0, keepdims=True).astype(jnp.int32)
        at_slot = (lax.broadcasted_iota(jnp.int32, (LANES, rows), 0) == slot).astype(jnp.float32)
        high = (row // 16).astype(jnp.float32)
        low = (row % 16).astype(jnp.float32)
        contract = (((1,), (1,)), ((), ()))
        high_part = lax.dot_general(
            named16, (at_slot * high).astype(jnp.bfloat16), contract,
            preferred_element_type=jnp.float32,
        )
        low_part = lax.dot_general(
            named16, (at_slot * low).astype(jnp.bfloat16), contract,
            preferred_element_type=jnp.float32,
        )
        request_ref[side] = (16.0 * high_part + low_part).astype(jnp.int32)
        place_ref[side : side + 1, :] = side * slabs * CAP + peer * CAP + slot


def displaced(slab, number):
    phase = number % 8
    wave = number // 8
    shift_z = jnp.where(phase % 2 == 0, (8 - phase // 2) % 8, (phase + 1) // 2)
    shift_x = 2 * (wave % 2) + wave // 4
    shift_c = (wave // 2) % 2
    core = (slab % 2 + shift_c) % 2
    at_x = ((slab // 2) % 4 + shift_x) % 4
    at_z = (slab // 8 + shift_z) % 8
    return (at_z * 4 + at_x) * 2 + core


def exchange_kernel(
    request_ref, volume_ref, arrived_ref,
    asked, asked_scalar, by_row, packed, relay,
    ask_send, ask_recv, local_sem, row_send, row_recv, relay_recv, relay_send,
):
    scan = lax.axis_index("scan")
    slab = lax.axis_index("slab")
    slabs = request_ref.shape[1]
    rows = volume_ref.shape[0]
    last = 3
    edge = jnp.logical_or(scan == 0, scan == last)
    inner_down = scan >= 1
    inner_up = scan <= last - 1

    barrier = pltpu.get_barrier_semaphore()

    def greet(number, carry):
        @pl.when(inner_down)
        def _():
            pl.semaphore_signal(barrier, inc=1, device_id=(scan - 1, number), device_id_type=MESH)

        @pl.when(inner_up)
        def _():
            pl.semaphore_signal(barrier, inc=1, device_id=(scan + 1, number), device_id_type=MESH)

        @pl.when(jnp.logical_and(edge, number != slab))
        def _():
            pl.semaphore_signal(barrier, inc=1, device_id=(scan, number), device_id_type=MESH)

        return carry

    lax.fori_loop(0, slabs, greet, 0)

    def relayout(block, carry):
        base = pl.multiple_of(block * 8, 8)
        for part in range(8):
            by_row[pl.ds(base, 8), part, :] = volume_ref[
                pl.ds(base, 8), part * LANES : (part + 1) * LANES
            ]
        return carry

    lax.fori_loop(0, rows // 8, relayout, 0)
    pl.semaphore_wait(barrier, jnp.where(edge, 2 * slabs - 1, 2 * slabs))

    def ask_copy(side, number):
        return pltpu.make_async_remote_copy(
            src_ref=request_ref.at[side, number],
            dst_ref=asked.at[side, slab],
            send_sem=ask_send.at[side],
            recv_sem=ask_recv.at[side],
            device_id=(scan + 1 - 2 * side, number),
            device_id_type=MESH,
        )

    def ask(number, carry):
        target = displaced(slab, number)

        @pl.when(inner_up)
        def _():
            ask_copy(0, target).start()

        @pl.when(inner_down)
        def _():
            ask_copy(1, target).start()

        return carry

    lax.fori_loop(0, slabs, ask, 0)

    def whole_ask(side):
        return pltpu.make_async_remote_copy(
            src_ref=request_ref.at[side],
            dst_ref=asked.at[side],
            send_sem=ask_send.at[side],
            recv_sem=ask_recv.at[side],
            device_id=(scan, slab),
            device_id_type=MESH,
        )

    def take_asked(side):
        whole_ask(side).wait_recv()
        copy = pltpu.make_async_copy(asked.at[side], asked_scalar.at[side], local_sem)
        copy.start()
        copy.wait()

    @pl.when(inner_down)
    def _():
        take_asked(0)

    @pl.when(inner_up)
    def _():
        take_asked(1)

    def pack(side, number, target):
        for slot in range(CAP):
            row = asked_scalar[side, target, 0, slot]
            packed[side, number, slot] = by_row[row]

    def row_copy(source, side, target, target_scan, send_sem):
        return pltpu.make_async_remote_copy(
            src_ref=source,
            dst_ref=arrived_ref.at[side, slab],
            send_sem=send_sem,
            recv_sem=row_recv.at[side],
            device_id=(target_scan, target),
            device_id_type=MESH,
        )

    def relay_copy(side, number, relay_number, target_scan):
        return pltpu.make_async_remote_copy(
            src_ref=packed.at[side, number],
            dst_ref=relay.at[relay_number],
            send_sem=row_send.at[side],
            recv_sem=relay_recv.at[relay_number],
            device_id=(target_scan, slab),
            device_id_type=MESH,
        )

    def serve(side, number, target, relayed_scan):
        target_scan = scan - 1 + 2 * side
        relay_number = (number // 16) * 8 + number % 8
        relayed = jnp.logical_and(scan == relayed_scan, (number // 8) % 2 == 1)
        pack(side, number, target)

        @pl.when(relayed)
        def _():
            relay_copy(side, number, relay_number, target_scan).start()

        @pl.when(jnp.logical_not(relayed))
        def _():
            row_copy(packed.at[side, number], side, target, target_scan, row_send.at[side]).start()

    def send(number, carry):
        target = displaced(slab, number)

        @pl.when(inner_down)
        def _():
            serve(0, number, target, 1)

        @pl.when(inner_up)
        def _():
            serve(1, number, target, 2)

        return carry

    lax.fori_loop(0, slabs, send, 0)

    def pass_on(side):
        def forward(relay_number, carry):
            number = (relay_number // 8) * 16 + 8 + relay_number % 8
            pltpu.make_async_remote_copy(
                src_ref=relay.at[relay_number],
                dst_ref=relay.at[relay_number],
                send_sem=relay_send,
                recv_sem=relay_recv.at[relay_number],
                device_id=(scan, slab),
                device_id_type=MESH,
            ).wait_recv()
            row_copy(
                relay.at[relay_number], side, displaced(slab, number), scan, relay_send
            ).start()
            return carry

        lax.fori_loop(0, slabs // 2, forward, 0)

    @pl.when(scan == 0)
    def _():
        pass_on(0)

    @pl.when(scan == last)
    def _():
        pass_on(1)

    def whole_rows(side):
        return pltpu.make_async_remote_copy(
            src_ref=packed.at[side],
            dst_ref=arrived_ref.at[side],
            send_sem=row_send.at[side],
            recv_sem=row_recv.at[side],
            device_id=(scan, slab),
            device_id_type=MESH,
        )

    @pl.when(inner_up)
    def _():
        whole_ask(0).wait_send()
        whole_rows(1).wait_send()
        whole_rows(0).wait_recv()

    @pl.when(inner_down)
    def _():
        whole_ask(1).wait_send()
        whole_rows(0).wait_send()
        whole_rows(1).wait_recv()

    @pl.when(edge)
    def _():
        pltpu.make_async_remote_copy(
            src_ref=relay,
            dst_ref=relay,
            send_sem=relay_send,
            recv_sem=relay_recv.at[0],
            device_id=(scan, slab),
            device_id_type=MESH,
        ).wait_send()


def filter_parts():
    source = np.arange(LANES)[:, None]
    column = np.arange(2 * LANES)[None, :]
    lane = column % LANES
    beside = np.where(lane < LANES // 2, lane + LANES, lane - LANES)
    distance = np.abs(source - np.where(column < LANES, lane, beside))
    matrix = np.where(distance <= BAND, root_three * pole_value ** distance, 0.0)
    matrix = matrix.astype(np.float32)
    high = matrix.astype(jnp.bfloat16)
    low = (matrix - high.astype(np.float32)).astype(jnp.bfloat16)
    return jnp.asarray(high), jnp.asarray(low)


def terms_kernel(
    place_ref, arrived_ref, volume_ref, high_ref, low_ref,
    moment_ref, part0_ref, part1_ref, part2_ref, gathered, middle, beside, partial,
):
    rows = volume_ref.shape[0]
    parts = volume_ref.shape[1] // LANES
    scan = lax.axis_index("scan")
    first_row = pl.program_id(0) * rows
    lane = lax.broadcasted_iota(jnp.int32, (8, LANES), 1)

    for side in range(2):
        def fetch(group, carry):
            for one in range(8):
                row = group * 8 + one
                place = place_ref[side, first_row + row]
                gathered[side, pl.ds(pl.multiple_of(row * 8, 8), 8), :] = arrived_ref[
                    pl.ds(pl.multiple_of(place * 8, 8), 8), :
                ]
            return carry

        lax.fori_loop(0, rows // 8, fetch, 0)
        present = (scan <= 2) if side == 0 else (scan >= 1)
        for part in range(parts):
            voxels = gathered[side, pl.ds(part, rows, stride=parts), :]
            voxels = jnp.where(present, voxels, 0.0)
            top = voxels.astype(jnp.bfloat16)
            rest = (voxels - top.astype(jnp.float32)).astype(jnp.bfloat16)
            both = (
                jnp.dot(top, high_ref[...], preferred_element_type=jnp.float32)
                + jnp.dot(rest, high_ref[...], preferred_element_type=jnp.float32)
                + jnp.dot(top, low_ref[...], preferred_element_type=jnp.float32)
            )
            middle[side, part] = both[:, :LANES]
            beside[side, part] = both[:, LANES:]

    zero = jnp.zeros((8, LANES), jnp.float32)

    def combine(group, carry):
        at = pl.ds(pl.multiple_of(group * 8, 8), 8)
        values, slopes, bends = [], [], []
        for side in range(2):
            coeffs = []
            for part in range(parts):
                left = beside[side, part - 1, at, :] if part > 0 else zero
                right = beside[side, part + 1, at, :] if part < parts - 1 else zero
                coeffs.append(middle[side, part, at, :] + jnp.where(lane < LANES // 2, left, right))
            to_right = [pltpu.roll(one, 1, 1) for one in coeffs]
            to_left = [pltpu.roll(one, LANES - 1, 1) for one in coeffs]
            value, slope, bend = [], [], []
            for part in range(parts):
                before = jnp.where(lane == 0, to_right[part - 1] if part > 0 else zero, to_right[part])
                after = jnp.where(
                    lane == LANES - 1, to_left[part + 1] if part < parts - 1 else zero, to_left[part]
                )
                ends = before + after
                value.append((ends + 4.0 * coeffs[part]) * (1.0 / 6.0))
                slope.append(0.5 * (after - before))
                bend.append(ends - 2.0 * coeffs[part])
            values.append(value)
            slopes.append(slope)
            bends.append(bend)
        sums = [zero] * 5
        for part in range(parts):
            columns = slice(part * LANES, (part + 1) * LANES)
            voxels = volume_ref[at, columns]
            off_f = values[0][part] - voxels
            off_b = values[1][part] - voxels
            slope_f, slope_b = slopes[0][part], slopes[1][part]
            bend_f, bend_b = bends[0][part], bends[1][part]
            sums[0] += slope_f * off_f - slope_b * off_b
            sums[1] += bend_f * off_f + bend_b * off_b
            sums[2] += slope_f * slope_f + slope_b * slope_b
            sums[3] += slope_f * bend_f - slope_b * bend_b
            sums[4] += bend_f * bend_f + bend_b * bend_b
            part0_ref[at, columns] = off_f + off_b
            part1_ref[at, columns] = slope_f - slope_b
            part2_ref[at, columns] = 0.5 * (bend_f + bend_b)
        for number in range(5):
            partial[number, at, :] = sums[number]
        return carry

    lax.fori_loop(0, rows // 8, combine, 0)
    ones = jnp.ones((8, LANES), jnp.float32)
    for number in range(5):
        total = lax.dot_general(
            ones, partial[number], (((1,), (1,)), ((), ())),
            preferred_element_type=jnp.float32, precision=lax.Precision.HIGHEST,
        )
        moment_ref[number : number + 1, :] = total[0:1, :]


def descent_kernel(
    table_ref, moment_ref, velocity_ref, class_ref, out_ref,
    fields, halos, totals, near_box, far_box,
    halo_send, halo_recv, near_send, near_recv, far_send, far_recv,
):
    scan = lax.axis_index("scan")
    slab = lax.axis_index("slab")
    rows = velocity_ref.shape[1]
    slabs = 64
    scans = 4
    layers = 8
    group = slabs // layers
    place = slab % group
    layer = slab // group
    fars = scans * layers
    own_far = scan * layers + layer
    steps = ((-1, slab >= 1), (1, slab <= slabs - 2), (-2, slab >= 2), (2, slab <= slabs - 3))

    def near_peer(number):
        return (scan, layer * group + (place + 1 + number) % group)

    def far_peer(number):
        other = (own_far + 1 + number) % fars
        return (other // layers, (other % layers) * group + place)

    barrier = pltpu.get_barrier_semaphore()
    expected = group - 1 + fars - 1
    for step, exists in steps:
        @pl.when(exists)
        def _():
            pl.semaphore_signal(barrier, inc=1, device_id=(scan, slab + step), device_id_type=MESH)

        expected = expected + jnp.where(exists, 1, 0)

    def greet_near(number, carry):
        pl.semaphore_signal(barrier, inc=1, device_id=near_peer(number), device_id_type=MESH)
        return carry

    def greet_far(number, carry):
        pl.semaphore_signal(barrier, inc=1, device_id=far_peer(number), device_id_type=MESH)
        return carry

    lax.fori_loop(0, group - 1, greet_near, 0)
    lax.fori_loop(0, fars - 1, greet_far, 0)

    weight = jnp.zeros((1, rows), jnp.float32)
    for number in range(4):
        weight = jnp.where(class_ref[...] == number, table_ref[number], weight)
    stiffness = jnp.sqrt(weight)
    velocity = velocity_ref[...]
    lane = lax.broadcasted_iota(jnp.int32, (1, rows), 1)
    pl.semaphore_wait(barrier, expected)

    def halo_copy(turn, number, step):
        return pltpu.make_async_remote_copy(
            src_ref=fields.at[turn],
            dst_ref=halos.at[turn, number],
            send_sem=halo_send.at[turn, number],
            recv_sem=halo_recv.at[turn, number],
            device_id=(scan, slab + step),
            device_id_type=MESH,
        )

    sources = (slab <= slabs - 2, slab >= 1, slab <= slabs - 3, slab >= 2)

    def stencil(turn, field):
        fields[turn] = field
        for number, (step, exists) in enumerate(steps):
            @pl.when(exists)
            def _():
                halo_copy(turn, number, step).start()

        for number, (step, exists) in enumerate(steps):
            @pl.when(sources[number])
            def _():
                halo_copy(turn, number, step).wait_recv()

        got = [jnp.where(sources[number], halos[turn, number], 0.0) for number in range(4)]
        before = jnp.where(lane == 0, pltpu.roll(got[1], 1, 1), pltpu.roll(field, 1, 1))
        after = jnp.where(lane == rows - 1, pltpu.roll(got[0], rows - 1, 1), pltpu.roll(field, rows - 1, 1))
        for number, (step, exists) in enumerate(steps):
            @pl.when(exists)
            def _():
                halo_copy(turn, number, step).wait_send()

        return 4.0 * field - before - after - got[2] - got[3]

    def summed(turn, mine):
        totals[turn, 0] = mine

        def near_copy(number):
            return pltpu.make_async_remote_copy(
                src_ref=totals.at[turn, 0],
                dst_ref=near_box.at[turn, number],
                send_sem=near_send.at[turn, number],
                recv_sem=near_recv.at[turn, number],
                device_id=near_peer(number),
                device_id_type=MESH,
            )

        for number in range(group - 1):
            near_copy(number).start()
        for number in range(group - 1):
            near_copy(number).wait()
        mine = mine + jnp.sum(near_box[turn], axis=0)
        totals[turn, 1] = mine

        def far_copy(number):
            return pltpu.make_async_remote_copy(
                src_ref=totals.at[turn, 1],
                dst_ref=far_box.at[turn, number],
                send_sem=far_send.at[turn, number],
                recv_sem=far_recv.at[turn, number],
                device_id=far_peer(number),
                device_id_type=MESH,
            )

        def start(number, carry):
            far_copy(number).start()
            return carry

        def wait(number, carry):
            far_copy(number).wait()
            return carry

        lax.fori_loop(0, fars - 1, start, 0)
        lax.fori_loop(0, fars - 1, wait, 0)
        mine = mine + jnp.sum(far_box[turn], axis=0)
        upper = jnp.sum(mine[:, :LANES], axis=1, keepdims=True)
        lower = jnp.sum(mine[:, LANES:], axis=1, keepdims=True)
        return upper / lower

    def folded(values):
        return sum(values[:, at : at + LANES] for at in range(0, rows, LANES))

    m0, m1, m2, m3, m4 = (moment_ref[number : number + 1, :] for number in range(5))
    smooth = stencil(0, stiffness * velocity)
    for turn in range(ITERS):
        linear = m0 + velocity * (m1 + m2) + 1.5 * velocity * velocity * m3 + (
            0.5 * velocity * velocity * velocity * m4
        )
        curvature = m2 + 2.0 * velocity * m3 + velocity * velocity * m4
        gradient = linear + stiffness * smooth
        direction = gradient / (curvature + 4.0 * stiffness * stiffness)
        scaled = stiffness * direction
        bent = stencil(turn + 1, scaled)
        mine = jnp.concatenate(
            [
                folded(direction * gradient),
                folded(curvature * direction * direction + scaled * bent),
            ],
            axis=1,
        )
        alpha = summed(turn, mine)
        velocity = velocity - alpha * direction
        smooth = smooth - alpha * bent
    out_ref[...] = velocity


def misfit_kernel(velocity_ref, part0_ref, part1_ref, part2_ref, out_ref, velocity_out_ref):
    rows = out_ref.shape[0]
    across = velocity_ref[...]
    velocity_out_ref[...] = across
    down = jnp.transpose(jnp.broadcast_to(across, (rows, rows)))
    for at in range(0, out_ref.shape[1], LANES):
        columns = slice(at, at + LANES)
        out_ref[:, columns] = part0_ref[:, columns] + down * (
            part1_ref[:, columns] + down * part2_ref[:, columns]
        )


def on_device(volume, velocity0, fetch_slab, fetch_row, modulus_class, modulus_table):
    rows, length = volume.shape[1:]
    slabs = 64
    parts = length // LANES
    f32 = jnp.float32
    vmem = pl.BlockSpec(memory_space=pltpu.VMEM)
    smem = pl.BlockSpec(memory_space=pltpu.SMEM)
    own_scan = volume.reshape(rows, length)
    peer = fetch_slab.reshape(2, rows)
    row = fetch_row.reshape(2, rows)
    dma = pltpu.SemaphoreType.DMA

    request, place = pl.pallas_call(
        slots_kernel,
        name="slots",
        out_shape=(
            jax.ShapeDtypeStruct((2, slabs, LANES), jnp.int32),
            jax.ShapeDtypeStruct((2, rows), jnp.int32),
        ),
        in_specs=[vmem, vmem],
        out_specs=(vmem, vmem),
    )(peer, row)

    arrived = pl.pallas_call(
        exchange_kernel,
        name="exchange",
        out_shape=jax.ShapeDtypeStruct((2, slabs, CAP, parts, LANES), f32),
        in_specs=[vmem, vmem],
        out_specs=pl.BlockSpec(memory_space=pl.ANY),
        scratch_shapes=[
            pltpu.VMEM((2, slabs, 1, LANES), jnp.int32),
            pltpu.SMEM((2, slabs, 1, LANES), jnp.int32),
            pltpu.VMEM((rows, parts, LANES), f32),
            pltpu.VMEM((2, slabs, CAP, parts, LANES), f32),
            pltpu.VMEM((slabs // 2, CAP, parts, LANES), f32),
            dma((2,)), dma((2,)), dma, dma((2,)), dma((2,)), dma((slabs // 2,)), dma,
        ],
        compiler_params=pltpu.CompilerParams(
            collective_id=0, has_side_effects=True, vmem_limit_bytes=40 * 1024 * 1024
        ),
    )(request.reshape(2, slabs, 1, LANES), own_scan)

    high, low = filter_parts()
    block = 128
    columns = pl.BlockSpec((block, length), lambda step: (step, 0))
    moments, part0, part1, part2 = pl.pallas_call(
        terms_kernel,
        name="terms",
        grid=(rows // block,),
        out_shape=(
            jax.ShapeDtypeStruct((8, rows), f32),
            jax.ShapeDtypeStruct((rows, length), f32),
            jax.ShapeDtypeStruct((rows, length), f32),
            jax.ShapeDtypeStruct((rows, length), f32),
        ),
        in_specs=[smem, vmem, columns, vmem, vmem],
        out_specs=(
            pl.BlockSpec((8, block), lambda step: (0, step)), columns, columns, columns,
        ),
        scratch_shapes=[
            pltpu.VMEM((2, block * parts, LANES), f32),
            pltpu.VMEM((2, parts, block, LANES), f32),
            pltpu.VMEM((2, parts, block, LANES), f32),
            pltpu.VMEM((5, block, LANES), f32),
        ],
        compiler_params=pltpu.CompilerParams(vmem_limit_bytes=40 * 1024 * 1024),
    )(place, arrived.reshape(2 * slabs * CAP * parts, LANES), own_scan, high, low)

    velocity = pl.pallas_call(
        descent_kernel,
        name="descent",
        out_shape=jax.ShapeDtypeStruct((1, rows), f32),
        in_specs=[smem, vmem, vmem, vmem],
        out_specs=vmem,
        scratch_shapes=[
            pltpu.VMEM((ITERS + 1, 1, rows), f32),
            pltpu.VMEM((ITERS + 1, 4, 1, rows), f32),
            pltpu.VMEM((ITERS, 2, 1, 2 * LANES), f32),
            pltpu.VMEM((ITERS, 7, 1, 2 * LANES), f32),
            pltpu.VMEM((ITERS, 31, 1, 2 * LANES), f32),
            dma((ITERS + 1, 4)), dma((ITERS + 1, 4)),
            dma((ITERS, 7)), dma((ITERS, 7)), dma((ITERS, 31)), dma((ITERS, 31)),
        ],
        compiler_params=pltpu.CompilerParams(collective_id=1, has_side_effects=True),
    )(modulus_table, moments, velocity0, modulus_class)

    misfit, velocity = pl.pallas_call(
        misfit_kernel,
        name="misfit",
        grid=(rows // block,),
        out_shape=(
            jax.ShapeDtypeStruct((rows, length), f32),
            jax.ShapeDtypeStruct((1, rows), f32),
        ),
        in_specs=[
            pl.BlockSpec((1, block), lambda step: (0, step)), columns, columns, columns,
        ],
        out_specs=(columns, pl.BlockSpec((1, block), lambda step: (0, step))),
    )(velocity, part0, part1, part2)
    return velocity, misfit.reshape(volume.shape)


def solution(mesh):
    return jax.shard_map(
        on_device,
        mesh=mesh,
        in_specs=(
            P("scan", "slab", None),
            P("scan", "slab"),
            P("scan", None, "slab", None),
            P("scan", None, "slab"),
            P("scan", "slab"),
            P(),
        ),
        out_specs=(P("scan", "slab"), P("scan", "slab", None)),
        check_vma=False,
    )
```

```python
import math

import jax
import jax.numpy as jnp
import numpy as np
from jax import lax
from jax.experimental import pallas as pl
from jax.experimental.pallas import tpu as pltpu
from jax.sharding import PartitionSpec as P

BAND = 32
ITERS = 2
CAP = 12
LANES = 128
SCANS = 4
SLABS = 64
LAYERS = 8
BATCH = 4
MESH = pl.DeviceIdType.MESH
MIB = 1024 * 1024

root_three = math.sqrt(3.0)
pole_value = math.sqrt(3.0) - 2.0


def filter_parts():
    source = np.arange(LANES)[:, None]
    column = np.arange(2 * LANES)[None, :]
    lane = column % LANES
    beside = np.where(lane < LANES // 2, lane + LANES, lane - LANES)
    distance = np.abs(source - np.where(column < LANES, lane, beside))
    matrix = np.where(distance <= BAND, root_three * pole_value ** distance, 0.0)
    matrix = matrix.astype(np.float32)
    high = matrix.astype(jnp.bfloat16)
    low = (matrix - high.astype(np.float32)).astype(jnp.bfloat16)
    return jnp.asarray(np.concatenate([high, high])), jnp.asarray(low)


def shifts(number):
    phase = number % 8
    wave = number // 8
    shift_z = jnp.where(phase % 2 == 0, (8 - phase // 2) % 8, (phase + 1) // 2)
    return shift_z, 2 * (wave % 2) + wave // 4, (wave // 2) % 2


def displaced(slab, number):
    shift_z, shift_x, shift_c = shifts(number)
    core = (slab % 2 + shift_c) % 2
    at_x = ((slab // 2) % 4 + shift_x) % 4
    at_z = (slab // 8 + shift_z) % 8
    return (at_z * 4 + at_x) * 2 + core


def number_between(source, target):
    shift_c = (target % 2 + 2 - source % 2) % 2
    shift_x = ((target // 2) % 4 + 4 - (source // 2) % 4) % 4
    shift_z = (target // 8 + 8 - source // 8) % 8
    phase = jnp.where(shift_z > 4, 2 * (8 - shift_z), jnp.maximum(2 * shift_z - 1, 0))
    wave = shift_x // 2 + 2 * shift_c + 4 * (shift_x % 2)
    return wave * 8 + phase


def slots_kernel(peer_ref, row_ref, request_ref, wanting_ref, place_ref):
    slab = lax.axis_index("slab")
    rows = peer_ref.shape[1]
    earlier = (
        lax.broadcasted_iota(jnp.int32, (rows, rows), 0)
        < lax.broadcasted_iota(jnp.int32, (rows, rows), 1)
    ).astype(jnp.float32).astype(jnp.bfloat16)
    contract = (((1,), (1,)), ((), ()))
    here = lax.broadcasted_iota(jnp.int32, (1, rows), 1)
    for side in range(2):
        peer = peer_ref[side : side + 1, :]
        named = (lax.broadcasted_iota(jnp.int32, (SLABS, rows), 0) == peer).astype(jnp.float32)
        named16 = named.astype(jnp.bfloat16)
        before = jnp.dot(named16, earlier, preferred_element_type=jnp.float32)
        slot = jnp.sum(before * named, axis=0, keepdims=True).astype(jnp.int32)
        at_slot = (lax.broadcasted_iota(jnp.int32, (LANES, rows), 0) == slot).astype(jnp.float32)

        def tabled(numbers):
            high = (at_slot * (numbers // 16).astype(jnp.float32)).astype(jnp.bfloat16)
            low = (at_slot * (numbers % 16).astype(jnp.float32)).astype(jnp.bfloat16)
            return (
                16.0 * lax.dot_general(named16, high, contract, preferred_element_type=jnp.float32)
                + lax.dot_general(named16, low, contract, preferred_element_type=jnp.float32)
            ).astype(jnp.int32)

        request_ref[side] = tabled(row_ref[side : side + 1, :])
        wanting_ref[side] = tabled(here)
        place_ref[side : side + 1, :] = number_between(peer, slab) * CAP + jnp.minimum(slot, CAP - 1)


def velocity_kernel(
    table_ref, wanting_scalar, place_scalar, request, place, volume_ref, velocity_ref, class_ref,
    high_ref, low_ref,
    out_ref, part0_ref, part1_ref, part2_ref,
    volume, by_row, asked, asked_scalar,
    packed, relay, arrived, value, slope, bend, middle, beside, own, sums, chosen, parts_buf,
    near_box, far_box, totals,
    volume_sem, ask_send, ask_recv, scalar_sem, row_send, row_recv, relay_recv, relay_send,
    near_send, near_recv, far_send, far_recv, part_sem,
):
    scan = lax.axis_index("scan")
    slab = lax.axis_index("slab")
    rows = velocity_ref.shape[1]
    blocks = volume_ref.shape[1] // LANES
    group = SLABS // LAYERS
    position = slab % group
    layer = slab // group
    fars = SCANS * LAYERS
    last = SCANS - 1
    edge = jnp.logical_or(scan == 0, scan == last)
    down = scan >= 1
    up = scan <= last - 1
    present = (up, down)

    volume_copy = pltpu.make_async_copy(volume_ref, volume, volume_sem)
    volume_copy.start()

    barrier = pltpu.get_barrier_semaphore()

    def near_peer(number):
        return (scan, layer * group + (position + 1 + number) % group)

    def far_peer(number):
        other = (scan * LAYERS + layer + 1 + number) % fars
        return (other // LAYERS, (other % LAYERS) * group + position)

    below = jnp.logical_and(layer >= 1, position <= 1)
    above = layer <= LAYERS - 2
    to_above = jnp.logical_and(above, position >= group - 2)

    def greet(device):
        pl.semaphore_signal(barrier, inc=1, device_id=device, device_id_type=MESH)

    def greet_rows(number, carry):
        @pl.when(down)
        def _():
            greet((scan - 1, number))

        @pl.when(up)
        def _():
            greet((scan + 1, number))

        @pl.when(jnp.logical_and(edge, number != slab))
        def _():
            greet((scan, number))

        return carry

    def greet_far(number, carry):
        greet(far_peer(number))
        return carry

    lax.fori_loop(0, SLABS, greet_rows, 0)
    lax.fori_loop(0, fars - 1, greet_far, 0)
    for number in range(group - 1):
        greet(near_peer(number))

    @pl.when(above)
    def _():
        for number in range(2):
            greet((scan, (layer + 1) * group + number))

    @pl.when(below)
    def _():
        for number in range(group):
            greet((scan, (layer - 1) * group + number))

    expected = (
        jnp.where(edge, 2 * SLABS - 1, 2 * SLABS) + fars - 1 + group - 1
        + jnp.where(above, 2, 0) + jnp.where(below, group, 0)
    )

    volume_copy.wait()

    def relayout(block, carry):
        base = pl.multiple_of(block * 8, 8)
        for part in range(blocks):
            by_row[pl.ds(base, 8), part, :] = volume[
                pl.ds(base, 8), part * LANES : (part + 1) * LANES
            ]
        return carry

    lax.fori_loop(0, rows // 8, relayout, 0)
    pl.semaphore_wait(barrier, expected)

    def ask_copy(side, number):
        return pltpu.make_async_remote_copy(
            src_ref=request.at[side, number],
            dst_ref=asked.at[side, slab],
            send_sem=ask_send.at[side],
            recv_sem=ask_recv.at[side],
            device_id=(scan + 1 - 2 * side, number),
            device_id_type=MESH,
        )

    def ask(number, carry):
        target = displaced(slab, number)

        @pl.when(up)
        def _():
            ask_copy(0, target).start()

        @pl.when(down)
        def _():
            ask_copy(1, target).start()

        return carry

    lax.fori_loop(0, SLABS, ask, 0)

    def whole_ask(side):
        return pltpu.make_async_remote_copy(
            src_ref=request.at[side],
            dst_ref=asked.at[side],
            send_sem=ask_send.at[side],
            recv_sem=ask_recv.at[side],
            device_id=(scan, slab),
            device_id_type=MESH,
        )

    def near_copy(turn, index, entry, device):
        return pltpu.make_async_remote_copy(
            src_ref=near_box.at[turn, position + 2],
            dst_ref=near_box.at[turn, entry],
            send_sem=near_send.at[turn, index],
            recv_sem=near_recv.at[turn, entry],
            device_id=device,
            device_id_type=MESH,
        )

    def shares(turn, act):
        for number in range(group - 1):
            act(near_copy(turn, number, position + 2, near_peer(number)))

        @pl.when(below)
        def _():
            for number in range(group):
                act(near_copy(turn, 7 + number, position + group + 2, (scan, (layer - 1) * group + number)))

        @pl.when(to_above)
        def _():
            for number in range(2):
                act(near_copy(turn, 7 + number, position - group + 2, (scan, (layer + 1) * group + number)))

    def share(turn, message):
        near_box[turn, position + 2] = message
        shares(turn, lambda copy: copy.start())

    def collect(turn):
        def wait(entry):
            near_copy(turn, 0, entry, (scan, slab)).wait_recv()

        for entry in range(2, group + 2):
            @pl.when(position + 2 != entry)
            def _():
                wait(entry)

        @pl.when(above)
        def _():
            wait(group + 2)
            wait(group + 3)

        @pl.when(below)
        def _():
            wait(0)
            wait(1)

        shares(turn, lambda copy: copy.wait_send())

    lane_row = lax.broadcasted_iota(jnp.int32, (1, rows), 1)

    def stencil(turn, field):
        def entry(offset):
            return near_box[turn, position + 2 + offset, :, :rows]

        lower1 = jnp.where(slab >= 1, entry(-1), 0.0)
        lower2 = jnp.where(slab >= 2, entry(-2), 0.0)
        upper1 = jnp.where(slab <= SLABS - 2, entry(1), 0.0)
        upper2 = jnp.where(slab <= SLABS - 3, entry(2), 0.0)
        left = jnp.where(lane_row == 0, pltpu.roll(lower1, 1, 1), pltpu.roll(field, 1, 1))
        right = jnp.where(
            lane_row == rows - 1, pltpu.roll(upper1, rows - 1, 1), pltpu.roll(field, rows - 1, 1)
        )
        return 4.0 * field - left - right - lower2 - upper2

    weight = jnp.zeros((1, rows), jnp.float32)
    for number in range(4):
        weight = jnp.where(class_ref[...] == number, table_ref[number], weight)
    stiffness = jnp.sqrt(weight)
    velocity = velocity_ref[...]
    blank = jnp.zeros((1, 2 * LANES), jnp.float32)
    share(0, jnp.concatenate([stiffness * velocity, blank], axis=1))

    def take_asked(side):
        whole_ask(side).wait_recv()
        copy = pltpu.make_async_copy(asked.at[side], asked_scalar.at[side], scalar_sem)
        copy.start()
        copy.wait()

    @pl.when(down)
    def _():
        take_asked(0)

    @pl.when(up)
    def _():
        take_asked(1)

    def row_copy(source, side, number, target, target_scan, send_sem):
        return pltpu.make_async_remote_copy(
            src_ref=source,
            dst_ref=arrived.at[side, number],
            send_sem=send_sem,
            recv_sem=row_recv.at[side, number],
            device_id=(target_scan, target),
            device_id_type=MESH,
        )

    def relay_copy(side, number, relay_number, target_scan):
        return pltpu.make_async_remote_copy(
            src_ref=packed.at[side, number],
            dst_ref=relay.at[relay_number],
            send_sem=row_send.at[side],
            recv_sem=relay_recv.at[relay_number],
            device_id=(target_scan, slab),
            device_id_type=MESH,
        )

    def serve(side, number, target, relayed_scan):
        target_scan = scan - 1 + 2 * side
        relay_number = (number // 16) * 8 + number % 8
        relayed = jnp.logical_and(scan == relayed_scan, (number // 8) % 2 == 1)
        for slot in range(CAP):
            packed[side, number, slot] = by_row[asked_scalar[side, target, 0, slot]]

        @pl.when(relayed)
        def _():
            relay_copy(side, number, relay_number, target_scan).start()

        @pl.when(jnp.logical_not(relayed))
        def _():
            row_copy(
                packed.at[side, number], side, number, target, target_scan, row_send.at[side]
            ).start()

    def send(number, carry):
        target = displaced(slab, number)

        @pl.when(down)
        def _():
            serve(0, number, target, 1)

        @pl.when(up)
        def _():
            serve(1, number, target, 2)

        return carry

    lax.fori_loop(0, SLABS, send, 0)

    for side in range(2):
        across = place[side : side + 1, :].astype(jnp.float32)
        upright = jnp.transpose(jnp.broadcast_to(across, (LANES, rows)))
        lane = lax.broadcasted_iota(jnp.int32, (rows, LANES), 1).astype(jnp.float32)
        for block in range(SLABS * CAP // LANES):
            at = side * SLABS * CAP + block * LANES
            chosen[:, at : at + LANES] = (
                (upright == lane + float(block * LANES)).astype(jnp.float32).astype(jnp.bfloat16)
            )

        @pl.when(jnp.logical_not(present[side]))
        def _():
            sums[side] = jnp.zeros(sums.shape[1:], jnp.float32)

    collect(0)
    smooth = stencil(0, stiffness * velocity)

    lane8 = lax.broadcasted_iota(jnp.int32, (8, LANES), 1)
    zero8 = jnp.zeros((8, LANES), jnp.float32)
    batch_rows = BATCH * CAP

    def absorb(side, batch):
        for one in range(BATCH):
            number = batch * BATCH + one
            row_copy(packed.at[side, number], side, number, slab, scan, row_send.at[side]).wait_recv()
        voxels = arrived[side, pl.ds(batch * BATCH, BATCH)].reshape(batch_rows * blocks, LANES)
        top = voxels.astype(jnp.bfloat16)
        rest = (voxels - top.astype(jnp.float32)).astype(jnp.bfloat16)
        both = jnp.dot(
            jnp.concatenate([top, rest], axis=1), high_ref[...], preferred_element_type=jnp.float32
        ) + jnp.dot(top, low_ref[...], preferred_element_type=jnp.float32)
        middle[...] = both[:, :LANES].reshape(batch_rows, blocks, LANES)
        beside[...] = both[:, LANES:].reshape(batch_rows, blocks, LANES)
        for chunk in range(BATCH):
            source = displaced_back(batch * BATCH + chunk)
            for slot in range(CAP):
                own[chunk * CAP + slot] = by_row[wanting_scalar[side, source, slot]]

        def combine(eight, carry):
            at = pl.ds(pl.multiple_of(eight * 8, 8), 8)
            to = pl.ds(pl.multiple_of(batch * batch_rows + eight * 8, 8), 8)
            coeffs = []
            for block in range(blocks):
                left = beside[at, block - 1, :] if block > 0 else zero8
                right = beside[at, block + 1, :] if block < blocks - 1 else zero8
                coeffs.append(middle[at, block, :] + jnp.where(lane8 < LANES // 2, left, right))
            to_right = [pltpu.roll(one, 1, 1) for one in coeffs]
            to_left = [pltpu.roll(one, LANES - 1, 1) for one in coeffs]
            total = [zero8] * 5
            for block in range(blocks):
                prior = jnp.where(lane8 == 0, to_right[block - 1] if block > 0 else zero8, to_right[block])
                after = jnp.where(
                    lane8 == LANES - 1,
                    to_left[block + 1] if block < blocks - 1 else zero8,
                    to_left[block],
                )
                ends = prior + after
                v = (ends + 4.0 * coeffs[block]) * (1.0 / 6.0)
                s = 0.5 * (after - prior)
                b = ends - 2.0 * coeffs[block]
                off = v - own[at, block, :]
                value[side, to, block, :] = v
                slope[side, to, block, :] = s
                bend[side, to, block, :] = b
                total[0] += s * off
                total[1] += b * off
                total[2] += s * s
                total[3] += s * b
                total[4] += b * b
            column = zero8
            for number in range(5):
                summed = jnp.sum(total[number], axis=1, keepdims=True)
                if side == 1 and number in (0, 3):
                    summed = -summed
                column = jnp.where(lane8 % 8 == number, summed, column)
            first = column.astype(jnp.bfloat16).astype(jnp.float32)
            second = (column - first).astype(jnp.bfloat16).astype(jnp.float32)
            third = (column - first - second).astype(jnp.bfloat16).astype(jnp.float32)
            column = jnp.where(lane8 < 8, first, jnp.where(lane8 < 16, second, third))
            sums[side, to, :] = jnp.where(lane8 < 24, column, 0.0)
            return carry

        lax.fori_loop(0, batch_rows // 8, combine, 0)

    def displaced_back(number):
        shift_z, shift_x, shift_c = shifts(number)
        core = (slab % 2 + 2 - shift_c) % 2
        at_x = ((slab // 2) % 4 + 4 - shift_x) % 4
        at_z = (slab // 8 + 8 - shift_z) % 8
        return (at_z * 4 + at_x) * 2 + core

    def pass_on(side, relay_number):
        number = (relay_number // 8) * 16 + 8 + relay_number % 8
        relay_copy(side, number, relay_number, scan).wait_recv()
        row_copy(
            relay.at[relay_number], side, number, displaced(slab, number), scan, relay_send
        ).start()

    def step(batch, carry):
        for side, relaying in ((0, scan == 0), (1, scan == last)):
            @pl.when(jnp.logical_and(relaying, batch < SLABS // 8))
            def _():
                for one in range(4):
                    pass_on(side, batch * 4 + one)

        for side in range(2):
            @pl.when(present[side])
            def _():
                absorb(side, batch)

        return carry

    lax.fori_loop(0, SLABS // BATCH, step, 0)

    moments = jnp.dot(
        chosen[...],
        sums[...].reshape(2 * SLABS * CAP, LANES).astype(jnp.bfloat16),
        preferred_element_type=jnp.float32,
    )
    moments = jnp.transpose(moments)
    moments = moments[0:8] + moments[8:16] + moments[16:24]
    m0, m1, m2, m3, m4 = (moments[number : number + 1, :] for number in range(5))

    def coefficients(quarter):
        def one_row(row):
            forward = place_scalar[0, row]
            backward = place_scalar[1, row]

            def got(ref):
                return (
                    jnp.where(up, ref[0, forward], 0.0),
                    jnp.where(down, ref[1, backward], 0.0),
                )

            value_f, value_b = got(value)
            slope_f, slope_b = got(slope)
            bend_f, bend_b = got(bend)
            parts_buf[0, row] = value_f + value_b - 2.0 * by_row[row]
            parts_buf[1, row] = slope_f - slope_b
            parts_buf[2, row] = 0.5 * (bend_f + bend_b)

        def four(step, carry):
            for one in range(4):
                one_row(quarter * (rows // 4) + step * 4 + one)
            return carry

        lax.fori_loop(0, rows // 16, four, 0)
        for copy in part_copies(quarter):
            copy.start()

    def part_copies(quarter):
        at = pl.ds(quarter * (rows // 4), rows // 4)
        return [
            pltpu.make_async_copy(parts_buf.at[number, at], ref.at[at], part_sem.at[number, quarter])
            for number, ref in enumerate((part0_ref, part1_ref, part2_ref))
        ]

    def folded(values):
        return sum(values[:, at : at + LANES] for at in range(0, rows, LANES))

    for turn in range(ITERS):
        linear = m0 + velocity * (m1 + m2) + 1.5 * velocity * velocity * m3 + (
            0.5 * velocity * velocity * velocity * m4
        )
        curvature = m2 + 2.0 * velocity * m3 + velocity * velocity * m4
        gradient = linear + stiffness * smooth
        direction = gradient / (curvature + 4.0 * stiffness * stiffness)
        scaled = stiffness * direction
        share(
            turn + 1,
            jnp.concatenate(
                [
                    scaled,
                    folded(direction * gradient),
                    folded(curvature * direction * direction + 4.0 * scaled * scaled),
                ],
                axis=1,
            ),
        )
        coefficients(2 * turn)
        collect(turn + 1)
        box = near_box[turn + 1, :, 0, :]
        fields = box[2 : group + 2, :rows]
        beyond = jnp.where(
            jnp.logical_or(above, lax.broadcasted_iota(jnp.int32, (4, rows), 0) < 2),
            box[group : group + 4, :rows], 0.0,
        )
        next1 = jnp.concatenate([box[3 : group + 2, :rows], beyond[2:3]], axis=0)
        next2 = jnp.concatenate([box[4 : group + 2, :rows], beyond[2:4]], axis=0)
        lane_all = lax.broadcasted_iota(jnp.int32, (group, rows), 1)
        right = jnp.where(
            lane_all == rows - 1, pltpu.roll(next1, rows - 1, 1), pltpu.roll(fields, rows - 1, 1)
        )
        cross = jnp.sum(folded(fields * (right + next2)), axis=0, keepdims=True)
        mine = jnp.sum(box[2 : group + 2, rows:], axis=0, keepdims=True)
        mine = mine - jnp.concatenate([jnp.zeros_like(cross), 2.0 * cross], axis=1)
        totals[turn] = mine

        def far_copy(number):
            return pltpu.make_async_remote_copy(
                src_ref=totals.at[turn],
                dst_ref=far_box.at[turn, number],
                send_sem=far_send.at[turn, number],
                recv_sem=far_recv.at[turn, number],
                device_id=far_peer(number),
                device_id_type=MESH,
            )

        def far_start(number, carry):
            far_copy(number).start()
            return carry

        def far_wait(number, carry):
            far_copy(number).wait()
            return carry

        lax.fori_loop(0, fars - 1, far_start, 0)
        bent = stencil(turn + 1, scaled)
        coefficients(2 * turn + 1)
        lax.fori_loop(0, fars - 1, far_wait, 0)
        mine = mine + jnp.sum(far_box[turn], axis=0)
        upper = jnp.sum(mine[:, :LANES], axis=1, keepdims=True)
        lower = jnp.sum(mine[:, LANES:], axis=1, keepdims=True)
        alpha = upper / lower
        velocity = velocity - alpha * direction
        smooth = smooth - alpha * bent
    out_ref[...] = velocity

    @pl.when(up)
    def _():
        whole_ask(0).wait_send()

    @pl.when(down)
    def _():
        whole_ask(1).wait_send()

    for side, serving in ((0, down), (1, up)):
        @pl.when(serving)
        def _():
            pltpu.make_async_remote_copy(
                src_ref=packed.at[side],
                dst_ref=arrived.at[side],
                send_sem=row_send.at[side],
                recv_sem=row_recv.at[side, 0],
                device_id=(scan, slab),
                device_id_type=MESH,
            ).wait_send()

    @pl.when(edge)
    def _():
        pltpu.make_async_remote_copy(
            src_ref=relay,
            dst_ref=relay,
            send_sem=relay_send,
            recv_sem=relay_recv.at[0],
            device_id=(scan, slab),
            device_id_type=MESH,
        ).wait_send()

    for quarter in range(4):
        for copy in part_copies(quarter):
            copy.wait()


def misfit_kernel(velocity_ref, part0_ref, part1_ref, part2_ref, out_ref, velocity_out_ref, upright):
    rows = out_ref.shape[0]
    across = velocity_ref[...]
    velocity_out_ref[...] = across
    upright[...] = jnp.transpose(jnp.broadcast_to(across, (rows, rows)))

    def eight(step, carry):
        at = pl.ds(pl.multiple_of(step * 8, 8), 8)
        moved = upright[at, :]
        for block in range(out_ref.shape[1] // LANES):
            out_ref[at, block * LANES : (block + 1) * LANES] = part0_ref[at, block, :] + moved * (
                part1_ref[at, block, :] + moved * part2_ref[at, block, :]
            )
        return carry

    lax.fori_loop(0, rows // 8, eight, 0, unroll=2)


def on_device(volume, velocity0, fetch_slab, fetch_row, modulus_class, modulus_table):
    rows, length = volume.shape[1:]
    blocks = length // LANES
    f32 = jnp.float32
    i32 = jnp.int32
    vmem = pl.BlockSpec(memory_space=pltpu.VMEM)
    smem = pl.BlockSpec(memory_space=pltpu.SMEM)
    anywhere = pl.BlockSpec(memory_space=pl.ANY)
    dma = pltpu.SemaphoreType.DMA
    high, low = filter_parts()
    tile = (blocks, LANES)
    turns = ITERS + 1
    wide = rows + 2 * LANES

    request, wanting, place = pl.pallas_call(
        slots_kernel,
        name="slots",
        out_shape=(
            jax.ShapeDtypeStruct((2, SLABS, LANES), i32),
            jax.ShapeDtypeStruct((2, SLABS, LANES), i32),
            jax.ShapeDtypeStruct((2, rows), i32),
        ),
        in_specs=[vmem, vmem],
        out_specs=(vmem, vmem, vmem),
    )(fetch_slab.reshape(2, rows), fetch_row.reshape(2, rows))

    velocity, part0, part1, part2 = pl.pallas_call(
        velocity_kernel,
        name="velocity",
        out_shape=(
            jax.ShapeDtypeStruct((1, rows), f32),
            jax.ShapeDtypeStruct((rows,) + tile, f32),
            jax.ShapeDtypeStruct((rows,) + tile, f32),
            jax.ShapeDtypeStruct((rows,) + tile, f32),
        ),
        in_specs=[smem, smem, smem, vmem, vmem, anywhere, vmem, vmem, vmem, vmem],
        out_specs=(vmem, anywhere, anywhere, anywhere),
        scratch_shapes=[
            pltpu.VMEM((rows, length), f32),
            pltpu.VMEM((rows,) + tile, f32),
            pltpu.VMEM((2, SLABS, 1, LANES), i32),
            pltpu.SMEM((2, SLABS, 1, LANES), i32),
            pltpu.VMEM((2, SLABS, CAP) + tile, f32),
            pltpu.VMEM((SLABS // 2, CAP) + tile, f32),
            pltpu.VMEM((2, SLABS, CAP) + tile, f32),
            pltpu.VMEM((2, SLABS * CAP) + tile, f32),
            pltpu.VMEM((2, SLABS * CAP) + tile, f32),
            pltpu.VMEM((2, SLABS * CAP) + tile, f32),
            pltpu.VMEM((BATCH * CAP,) + tile, f32),
            pltpu.VMEM((BATCH * CAP,) + tile, f32),
            pltpu.VMEM((BATCH * CAP,) + tile, f32),
            pltpu.VMEM((2, SLABS * CAP, LANES), f32),
            pltpu.VMEM((rows, 2 * SLABS * CAP), jnp.bfloat16),
            pltpu.VMEM((3, rows) + tile, f32),
            pltpu.VMEM((turns, 12, 1, wide), f32),
            pltpu.VMEM((ITERS, SCANS * LAYERS - 1, 1, 2 * LANES), f32),
            pltpu.VMEM((ITERS, 1, 2 * LANES), f32),
            dma, dma((2,)), dma((2,)), dma, dma((2,)), dma((2, SLABS)),
            dma((SLABS // 2,)), dma,
            dma((turns, 15)), dma((turns, 12)),
            dma((ITERS, SCANS * LAYERS - 1)), dma((ITERS, SCANS * LAYERS - 1)),
            dma((3, 4)),
        ],
        compiler_params=pltpu.CompilerParams(
            collective_id=0, has_side_effects=True, vmem_limit_bytes=56 * MIB
        ),
    )(
        modulus_table, wanting, place, request.reshape(2, SLABS, 1, LANES), place,
        volume.reshape(rows, length), velocity0, modulus_class, high, low,
    )

    block = 128
    across = pl.BlockSpec((1, block), lambda step: (0, step))
    tiles = pl.BlockSpec((block,) + tile, lambda step: (step, 0, 0))
    misfit, velocity = pl.pallas_call(
        misfit_kernel,
        name="misfit",
        grid=(rows // block,),
        out_shape=(
            jax.ShapeDtypeStruct((rows, length), f32),
            jax.ShapeDtypeStruct((1, rows), f32),
        ),
        in_specs=[across, tiles, tiles, tiles],
        out_specs=(pl.BlockSpec((block, length), lambda step: (step, 0)), across),
        scratch_shapes=[pltpu.VMEM((block, block), f32)],
    )(velocity, part0, part1, part2)
    return velocity, misfit.reshape(volume.shape)


def solution(mesh):
    return jax.shard_map(
        on_device,
        mesh=mesh,
        in_specs=(
            P("scan", "slab", None),
            P("scan", "slab"),
            P("scan", None, "slab", None),
            P("scan", None, "slab"),
            P("scan", "slab"),
            P(),
        ),
        out_specs=(P("scan", "slab"), P("scan", "slab", None)),
        check_vma=False,
    )
```

```python
import math

import jax
import jax.numpy as jnp
import numpy as np
from jax import lax
from jax.experimental import pallas as pl
from jax.experimental.pallas import tpu as pltpu
from jax.sharding import PartitionSpec as P

BAND = 32
ITERS = 2
CAP = 12
LANES = 128
SCANS = 4
SLABS = 64
LAYERS = 8
BATCH = 2
MESH = pl.DeviceIdType.MESH
MIB = 1024 * 1024

root_three = math.sqrt(3.0)
pole_value = math.sqrt(3.0) - 2.0


def filter_parts():
    source = np.arange(LANES)[:, None]
    column = np.arange(2 * LANES)[None, :]
    lane = column % LANES
    beside = np.where(lane < LANES // 2, lane + LANES, lane - LANES)
    distance = np.abs(source - np.where(column < LANES, lane, beside))
    matrix = np.where(distance <= BAND, root_three * pole_value ** distance, 0.0)
    matrix = matrix.astype(np.float32)
    high = matrix.astype(jnp.bfloat16)
    low = (matrix - high.astype(np.float32)).astype(jnp.bfloat16)
    return jnp.asarray(np.concatenate([high, high])), jnp.asarray(low)


def over(number, by):
    return lax.div(number, jnp.int32(by))


def left_of(number, by):
    return lax.rem(number, jnp.int32(by))


def shifts(number):
    phase = left_of(number, 8)
    wave = over(number, 8)
    half = over(phase + 1, 2)
    shift_z = jnp.where(left_of(phase, 2) == 0, left_of(8 - half, 8), half)
    return shift_z, 2 * left_of(wave, 2) + over(wave, 4), left_of(over(wave, 2), 2)


def displaced(slab, number):
    shift_z, shift_x, shift_c = shifts(number)
    core = left_of(left_of(slab, 2) + shift_c, 2)
    at_x = left_of(over(slab, 2) + shift_x, 4)
    at_z = left_of(over(slab, 8) + shift_z, 8)
    return (at_z * 4 + at_x) * 2 + core


def number_between(source, target):
    shift_c = (target % 2 + 2 - source % 2) % 2
    shift_x = ((target // 2) % 4 + 4 - (source // 2) % 4) % 4
    shift_z = (target // 8 + 8 - source // 8) % 8
    phase = jnp.where(shift_z > 4, 2 * (8 - shift_z), jnp.maximum(2 * shift_z - 1, 0))
    wave = shift_x // 2 + 2 * shift_c + 4 * (shift_x % 2)
    return wave * 8 + phase


def slots_kernel(peer_ref, row_ref, request_ref, wanting_ref, place_ref):
    slab = lax.axis_index("slab")
    rows = peer_ref.shape[1]
    earlier = (
        lax.broadcasted_iota(jnp.int32, (rows, rows), 0)
        < lax.broadcasted_iota(jnp.int32, (rows, rows), 1)
    ).astype(jnp.float32).astype(jnp.bfloat16)
    contract = (((1,), (1,)), ((), ()))
    here = lax.broadcasted_iota(jnp.int32, (1, rows), 1)
    for side in range(2):
        peer = peer_ref[side : side + 1, :]
        named = (lax.broadcasted_iota(jnp.int32, (SLABS, rows), 0) == peer).astype(jnp.float32)
        named16 = named.astype(jnp.bfloat16)
        before = jnp.dot(named16, earlier, preferred_element_type=jnp.float32)
        slot = jnp.sum(before * named, axis=0, keepdims=True).astype(jnp.int32)
        at_slot = (lax.broadcasted_iota(jnp.int32, (LANES, rows), 0) == slot).astype(jnp.float32)

        def tabled(numbers):
            high = (at_slot * (numbers // 16).astype(jnp.float32)).astype(jnp.bfloat16)
            low = (at_slot * (numbers % 16).astype(jnp.float32)).astype(jnp.bfloat16)
            return (
                16.0 * lax.dot_general(named16, high, contract, preferred_element_type=jnp.float32)
                + lax.dot_general(named16, low, contract, preferred_element_type=jnp.float32)
            ).astype(jnp.int32)

        request_ref[side] = tabled(row_ref[side : side + 1, :])
        wanting_ref[side] = tabled(here)
        place_ref[side : side + 1, :] = number_between(peer, slab) * CAP + jnp.minimum(slot, CAP - 1)


def velocity_kernel(
    table_ref, wanting_scalar, place_scalar, request, place, volume_ref, velocity_ref, class_ref,
    high_ref, low_ref,
    out_ref, part0_ref, part1_ref, part2_ref,
    volume, by_row, asked, asked_scalar,
    packed, relay, arrived, value, slope, bend, middle, beside, own, sums, chosen, parts_buf,
    turned, near_box, far_box, totals,
    volume_sem, ask_send, ask_recv, scalar_sem, row_send, row_recv, relay_recv, relay_send,
    near_send, near_recv, far_send, far_recv, part_sem,
):
    scan = lax.axis_index("scan")
    slab = lax.axis_index("slab")
    rows = velocity_ref.shape[1]
    blocks = volume_ref.shape[1] // LANES
    group = SLABS // LAYERS
    position = slab % group
    layer = slab // group
    fars = SCANS * LAYERS
    last = SCANS - 1
    edge = jnp.logical_or(scan == 0, scan == last)
    down = scan >= 1
    up = scan <= last - 1
    present = (up, down)

    volume_copy = pltpu.make_async_copy(volume_ref, volume, volume_sem)
    volume_copy.start()

    barrier = pltpu.get_barrier_semaphore()

    def near_peer(number):
        return (scan, layer * group + left_of(position + 1 + number, group))

    def far_peer(number):
        other = left_of(scan * LAYERS + layer + 1 + number, fars)
        return (over(other, LAYERS), left_of(other, LAYERS) * group + position)

    below = jnp.logical_and(layer >= 1, position <= 1)
    above = layer <= LAYERS - 2
    to_above = jnp.logical_and(above, position >= group - 2)

    def greet(device):
        pl.semaphore_signal(barrier, inc=1, device_id=device, device_id_type=MESH)

    def greet_rows(number, carry):
        @pl.when(down)
        def _():
            greet((scan - 1, number))

        @pl.when(up)
        def _():
            greet((scan + 1, number))

        @pl.when(jnp.logical_and(edge, number != slab))
        def _():
            greet((scan, number))

        return carry

    def greet_far(number, carry):
        greet(far_peer(number))
        return carry

    lax.fori_loop(0, SLABS, greet_rows, 0)
    lax.fori_loop(0, fars - 1, greet_far, 0)
    for number in range(group - 1):
        greet(near_peer(number))

    @pl.when(above)
    def _():
        for number in range(2):
            greet((scan, (layer + 1) * group + number))

    @pl.when(below)
    def _():
        for number in range(group):
            greet((scan, (layer - 1) * group + number))

    expected = (
        jnp.where(edge, 2 * SLABS - 1, 2 * SLABS) + fars - 1 + group - 1
        + jnp.where(above, 2, 0) + jnp.where(below, group, 0)
    )

    volume_copy.wait()

    def relayout(block, carry):
        base = pl.multiple_of(block * 8, 8)
        for part in range(blocks):
            by_row[pl.ds(base, 8), part, :] = volume[
                pl.ds(base, 8), part * LANES : (part + 1) * LANES
            ]
        return carry

    lax.fori_loop(0, rows // 8, relayout, 0)
    pl.semaphore_wait(barrier, expected)

    def ask_copy(side, number):
        return pltpu.make_async_remote_copy(
            src_ref=request.at[side, number],
            dst_ref=asked.at[side, slab],
            send_sem=ask_send.at[side],
            recv_sem=ask_recv.at[side],
            device_id=(scan + 1 - 2 * side, number),
            device_id_type=MESH,
        )

    def ask(number, carry):
        target = left_of(slab + number, SLABS)

        @pl.when(up)
        def _():
            ask_copy(0, target).start()

        @pl.when(down)
        def _():
            ask_copy(1, target).start()

        return carry

    lax.fori_loop(0, SLABS, ask, 0)

    def whole_ask(side):
        return pltpu.make_async_remote_copy(
            src_ref=request.at[side],
            dst_ref=asked.at[side],
            send_sem=ask_send.at[side],
            recv_sem=ask_recv.at[side],
            device_id=(scan, slab),
            device_id_type=MESH,
        )

    def near_copy(turn, index, entry, device):
        return pltpu.make_async_remote_copy(
            src_ref=near_box.at[turn, position + 2],
            dst_ref=near_box.at[turn, entry],
            send_sem=near_send.at[turn, index],
            recv_sem=near_recv.at[turn, entry],
            device_id=device,
            device_id_type=MESH,
        )

    def shares(turn, act):
        for number in range(group - 1):
            act(near_copy(turn, number, position + 2, near_peer(number)))

        @pl.when(below)
        def _():
            for number in range(group):
                act(near_copy(turn, 7 + number, position + group + 2, (scan, (layer - 1) * group + number)))

        @pl.when(to_above)
        def _():
            for number in range(2):
                act(near_copy(turn, 7 + number, position - group + 2, (scan, (layer + 1) * group + number)))

    def share(turn, message):
        near_box[turn, position + 2] = message
        shares(turn, lambda copy: copy.start())

    def collect(turn):
        def wait(entry):
            near_copy(turn, 0, entry, (scan, slab)).wait_recv()

        for entry in range(2, group + 2):
            @pl.when(position + 2 != entry)
            def _():
                wait(entry)

        @pl.when(above)
        def _():
            wait(group + 2)
            wait(group + 3)

        @pl.when(below)
        def _():
            wait(0)
            wait(1)

        shares(turn, lambda copy: copy.wait_send())

    lane_row = lax.broadcasted_iota(jnp.int32, (1, rows), 1)

    def stencil(turn, field):
        def entry(offset):
            return near_box[turn, position + 2 + offset, :, :rows]

        lower1 = jnp.where(slab >= 1, entry(-1), 0.0)
        lower2 = jnp.where(slab >= 2, entry(-2), 0.0)
        upper1 = jnp.where(slab <= SLABS - 2, entry(1), 0.0)
        upper2 = jnp.where(slab <= SLABS - 3, entry(2), 0.0)
        left = jnp.where(lane_row == 0, pltpu.roll(lower1, 1, 1), pltpu.roll(field, 1, 1))
        right = jnp.where(
            lane_row == rows - 1, pltpu.roll(upper1, rows - 1, 1), pltpu.roll(field, rows - 1, 1)
        )
        return 4.0 * field - left - right - lower2 - upper2

    weight = jnp.zeros((1, rows), jnp.float32)
    for number in range(4):
        weight = jnp.where(class_ref[...] == number, table_ref[number], weight)
    stiffness = jnp.sqrt(weight)
    velocity = velocity_ref[...]

    def scalar_copy(side):
        return pltpu.make_async_copy(asked.at[side], asked_scalar.at[side], scalar_sem.at[side])

    for side, serving in ((0, down), (1, up)):
        @pl.when(serving)
        def _():
            whole_ask(side).wait_recv()
            scalar_copy(side).start()

    for side, serving in ((0, down), (1, up)):
        @pl.when(serving)
        def _():
            scalar_copy(side).wait()

    def row_copy(source, side, number, target, target_scan, send_sem):
        return pltpu.make_async_remote_copy(
            src_ref=source,
            dst_ref=arrived.at[side, number],
            send_sem=send_sem,
            recv_sem=row_recv.at[side, number],
            device_id=(target_scan, target),
            device_id_type=MESH,
        )

    def relay_copy(side, number, relay_number, target_scan):
        return pltpu.make_async_remote_copy(
            src_ref=packed.at[side, number],
            dst_ref=relay.at[relay_number],
            send_sem=row_send.at[side],
            recv_sem=relay_recv.at[relay_number],
            device_id=(target_scan, slab),
            device_id_type=MESH,
        )

    def serve(side, number, target, relayed_scan):
        target_scan = scan - 1 + 2 * side
        relay_number = (number // 16) * 8 + number % 8
        relayed = jnp.logical_and(scan == relayed_scan, (number // 8) % 2 == 1)
        for slot in range(CAP):
            packed[side, number, slot] = by_row[asked_scalar[side, target, 0, slot]]

        @pl.when(relayed)
        def _():
            relay_copy(side, number, relay_number, target_scan).start()

        @pl.when(jnp.logical_not(relayed))
        def _():
            row_copy(
                packed.at[side, number], side, number, target, target_scan, row_send.at[side]
            ).start()

    def send(number, carry):
        target = displaced(slab, number)

        @pl.when(down)
        def _():
            serve(0, number, target, 1)

        @pl.when(up)
        def _():
            serve(1, number, target, 2)

        return carry

    lax.fori_loop(0, SLABS, send, 0)
    blank = jnp.zeros((1, 2 * LANES), jnp.float32)
    share(0, jnp.concatenate([stiffness * velocity, blank], axis=1))

    for side in range(2):
        across = place[side : side + 1, :].astype(jnp.float32)
        upright = jnp.transpose(jnp.broadcast_to(across, (LANES, rows)))
        lane = lax.broadcasted_iota(jnp.int32, (rows, LANES), 1).astype(jnp.float32)
        for block in range(SLABS * CAP // LANES):
            at = side * SLABS * CAP + block * LANES
            chosen[:, at : at + LANES] = (
                (upright == lane + float(block * LANES)).astype(jnp.float32).astype(jnp.bfloat16)
            )

        @pl.when(jnp.logical_not(present[side]))
        def _():
            sums[side] = jnp.zeros(sums.shape[1:], jnp.float32)

    lane8 = lax.broadcasted_iota(jnp.int32, (8, LANES), 1)
    zero8 = jnp.zeros((8, LANES), jnp.float32)
    batch_rows = BATCH * CAP

    def absorb(side, batch):
        for one in range(BATCH):
            number = batch * BATCH + one
            row_copy(packed.at[side, number], side, number, slab, scan, row_send.at[side]).wait_recv()
        voxels = arrived[side, pl.ds(batch * BATCH, BATCH)].reshape(batch_rows * blocks, LANES)
        top = voxels.astype(jnp.bfloat16)
        rest = (voxels - top.astype(jnp.float32)).astype(jnp.bfloat16)
        both = jnp.dot(
            jnp.concatenate([top, rest], axis=1), high_ref[...], preferred_element_type=jnp.float32
        ) + jnp.dot(top, low_ref[...], preferred_element_type=jnp.float32)
        middle[...] = both[:, :LANES].reshape(batch_rows, blocks, LANES)
        beside[...] = both[:, LANES:].reshape(batch_rows, blocks, LANES)
        for chunk in range(BATCH):
            source = displaced_back(batch * BATCH + chunk)
            for slot in range(CAP):
                own[chunk * CAP + slot] = by_row[wanting_scalar[side, source, slot]]

        def combine(eight, carry):
            at = pl.ds(pl.multiple_of(eight * 8, 8), 8)
            to = pl.ds(pl.multiple_of(batch * batch_rows + eight * 8, 8), 8)
            coeffs = []
            for block in range(blocks):
                left = beside[at, block - 1, :] if block > 0 else zero8
                right = beside[at, block + 1, :] if block < blocks - 1 else zero8
                coeffs.append(middle[at, block, :] + jnp.where(lane8 < LANES // 2, left, right))
            to_right = [pltpu.roll(one, 1, 1) for one in coeffs]
            to_left = [pltpu.roll(one, LANES - 1, 1) for one in coeffs]
            total = [zero8] * 5
            for block in range(blocks):
                prior = jnp.where(lane8 == 0, to_right[block - 1] if block > 0 else zero8, to_right[block])
                after = jnp.where(
                    lane8 == LANES - 1,
                    to_left[block + 1] if block < blocks - 1 else zero8,
                    to_left[block],
                )
                ends = prior + after
                v = (ends + 4.0 * coeffs[block]) * (1.0 / 6.0)
                s = 0.5 * (after - prior)
                b = ends - 2.0 * coeffs[block]
                off = v - own[at, block, :]
                value[side, to, block, :] = v
                slope[side, to, block, :] = s
                bend[side, to, block, :] = b
                total[0] += s * off
                total[1] += b * off
                total[2] += s * s
                total[3] += s * b
                total[4] += b * b
            column = zero8
            for number in range(5):
                summed = jnp.sum(total[number], axis=1, keepdims=True)
                if side == 1 and number in (0, 3):
                    summed = -summed
                column = jnp.where(lane8 % 8 == number, summed, column)
            first = column.astype(jnp.bfloat16).astype(jnp.float32)
            second = (column - first).astype(jnp.bfloat16).astype(jnp.float32)
            third = (column - first - second).astype(jnp.bfloat16).astype(jnp.float32)
            column = jnp.where(lane8 < 8, first, jnp.where(lane8 < 16, second, third))
            sums[side, to, :] = jnp.where(lane8 < 24, column, 0.0)
            return carry

        lax.fori_loop(0, batch_rows // 8, combine, 0)

    def displaced_back(number):
        shift_z, shift_x, shift_c = shifts(number)
        core = left_of(left_of(slab, 2) + 2 - shift_c, 2)
        at_x = left_of(over(slab, 2) + 4 - shift_x, 4)
        at_z = left_of(over(slab, 8) + 8 - shift_z, 8)
        return (at_z * 4 + at_x) * 2 + core

    def pass_on(side, relay_number):
        number = (relay_number // 8) * 16 + 8 + relay_number % 8
        relay_copy(side, number, relay_number, scan).wait_recv()
        row_copy(
            relay.at[relay_number], side, number, displaced(slab, number), scan, relay_send
        ).start()

    def step(batch, carry):
        for side, relaying in ((0, scan == 0), (1, scan == last)):
            @pl.when(jnp.logical_and(relaying, batch < SLABS // 8))
            def _():
                for one in range(4):
                    pass_on(side, batch * 4 + one)

        for side in range(2):
            @pl.when(present[side])
            def _():
                absorb(side, batch)

        return carry

    lax.fori_loop(0, SLABS // BATCH, step, 0)

    collect(0)
    smooth = stencil(0, stiffness * velocity)
    moments = jnp.dot(
        chosen[...],
        sums[...].reshape(2 * SLABS * CAP, LANES).astype(jnp.bfloat16),
        preferred_element_type=jnp.float32,
    )
    moments = jnp.transpose(moments)
    moments = moments[0:8] + moments[8:16] + moments[16:24]
    m0, m1, m2, m3, m4 = (moments[number : number + 1, :] for number in range(5))

    def coefficients(quarter):
        def one_row(row, at):
            forward = place_scalar[0, row]
            backward = place_scalar[1, row]

            def got(ref):
                return (
                    jnp.where(up, ref[0, forward], 0.0),
                    jnp.where(down, ref[1, backward], 0.0),
                )

            value_f, value_b = got(value)
            slope_f, slope_b = got(slope)
            bend_f, bend_b = got(bend)
            turned[0, at] = value_f + value_b - 2.0 * by_row[row]
            turned[1, at] = slope_f - slope_b
            turned[2, at] = 0.5 * (bend_f + bend_b)

        def eight(step, carry):
            base = pl.multiple_of(quarter * (rows // 4) + step * 8, 8)
            half = (step % 2) * 8
            for one in range(8):
                one_row(base + one, half + one)
            for number in range(3):
                for block in range(blocks):
                    parts_buf[number, pl.ds(base, 8), block * LANES : (block + 1) * LANES] = turned[
                        number, pl.ds(pl.multiple_of(half, 8), 8), block, :
                    ]
            return carry

        lax.fori_loop(0, rows // 32, eight, 0)
        for copy in part_copies(quarter):
            copy.start()

    def part_copies(quarter):
        at = pl.ds(quarter * (rows // 4), rows // 4)
        return [
            pltpu.make_async_copy(parts_buf.at[number, at], ref.at[at], part_sem.at[number, quarter])
            for number, ref in enumerate((part0_ref, part1_ref, part2_ref))
        ]

    def folded(values):
        return sum(values[:, at : at + LANES] for at in range(0, rows, LANES))

    for turn in range(ITERS):
        linear = m0 + velocity * (m1 + m2) + 1.5 * velocity * velocity * m3 + (
            0.5 * velocity * velocity * velocity * m4
        )
        curvature = m2 + 2.0 * velocity * m3 + velocity * velocity * m4
        gradient = linear + stiffness * smooth
        direction = gradient / (curvature + 4.0 * stiffness * stiffness)
        scaled = stiffness * direction
        share(
            turn + 1,
            jnp.concatenate(
                [
                    scaled,
                    folded(direction * gradient),
                    folded(curvature * direction * direction + 4.0 * scaled * scaled),
                ],
                axis=1,
            ),
        )
        coefficients(2 * turn)
        collect(turn + 1)
        box = near_box[turn + 1, :, 0, :]
        fields = box[2 : group + 2, :rows]
        beyond = jnp.where(
            jnp.logical_or(above, lax.broadcasted_iota(jnp.int32, (4, rows), 0) < 2),
            box[group : group + 4, :rows], 0.0,
        )
        next1 = jnp.concatenate([box[3 : group + 2, :rows], beyond[2:3]], axis=0)
        next2 = jnp.concatenate([box[4 : group + 2, :rows], beyond[2:4]], axis=0)
        lane_all = lax.broadcasted_iota(jnp.int32, (group, rows), 1)
        right = jnp.where(
            lane_all == rows - 1, pltpu.roll(next1, rows - 1, 1), pltpu.roll(fields, rows - 1, 1)
        )
        cross = jnp.sum(folded(fields * (right + next2)), axis=0, keepdims=True)
        mine = jnp.sum(box[2 : group + 2, rows:], axis=0, keepdims=True)
        mine = mine - jnp.concatenate([jnp.zeros_like(cross), 2.0 * cross], axis=1)
        totals[turn] = mine

        def far_copy(number):
            return pltpu.make_async_remote_copy(
                src_ref=totals.at[turn],
                dst_ref=far_box.at[turn, number],
                send_sem=far_send.at[turn, number],
                recv_sem=far_recv.at[turn, number],
                device_id=far_peer(number),
                device_id_type=MESH,
            )

        def far_start(number, carry):
            far_copy(number).start()
            return carry

        def far_wait(number, carry):
            far_copy(number).wait()
            return carry

        lax.fori_loop(0, fars - 1, far_start, 0)
        bent = stencil(turn + 1, scaled)
        coefficients(2 * turn + 1)
        lax.fori_loop(0, fars - 1, far_wait, 0)
        mine = mine + jnp.sum(far_box[turn], axis=0)
        upper = jnp.sum(mine[:, :LANES], axis=1, keepdims=True)
        lower = jnp.sum(mine[:, LANES:], axis=1, keepdims=True)
        alpha = upper / lower
        velocity = velocity - alpha * direction
        smooth = smooth - alpha * bent
    out_ref[...] = velocity

    @pl.when(up)
    def _():
        whole_ask(0).wait_send()

    @pl.when(down)
    def _():
        whole_ask(1).wait_send()

    for side, serving in ((0, down), (1, up)):
        @pl.when(serving)
        def _():
            pltpu.make_async_remote_copy(
                src_ref=packed.at[side],
                dst_ref=arrived.at[side],
                send_sem=row_send.at[side],
                recv_sem=row_recv.at[side, 0],
                device_id=(scan, slab),
                device_id_type=MESH,
            ).wait_send()

    @pl.when(edge)
    def _():
        pltpu.make_async_remote_copy(
            src_ref=relay,
            dst_ref=relay,
            send_sem=relay_send,
            recv_sem=relay_recv.at[0],
            device_id=(scan, slab),
            device_id_type=MESH,
        ).wait_send()

    for quarter in range(4):
        for copy in part_copies(quarter):
            copy.wait()


def misfit_kernel(velocity_ref, part0_ref, part1_ref, part2_ref, out_ref, velocity_out_ref):
    rows = out_ref.shape[0]
    across = velocity_ref[...]
    velocity_out_ref[...] = across
    moved = jnp.transpose(jnp.broadcast_to(across, (rows, rows)))
    for at in range(0, out_ref.shape[1], LANES):
        columns = slice(at, at + LANES)
        out_ref[:, columns] = part0_ref[:, columns] + moved * (
            part1_ref[:, columns] + moved * part2_ref[:, columns]
        )


def on_device(volume, velocity0, fetch_slab, fetch_row, modulus_class, modulus_table):
    rows, length = volume.shape[1:]
    blocks = length // LANES
    f32 = jnp.float32
    i32 = jnp.int32
    vmem = pl.BlockSpec(memory_space=pltpu.VMEM)
    smem = pl.BlockSpec(memory_space=pltpu.SMEM)
    anywhere = pl.BlockSpec(memory_space=pl.ANY)
    dma = pltpu.SemaphoreType.DMA
    high, low = filter_parts()
    tile = (blocks, LANES)
    turns = ITERS + 1
    wide = rows + 2 * LANES

    request, wanting, place = pl.pallas_call(
        slots_kernel,
        name="slots",
        out_shape=(
            jax.ShapeDtypeStruct((2, SLABS, LANES), i32),
            jax.ShapeDtypeStruct((2, SLABS, LANES), i32),
            jax.ShapeDtypeStruct((2, rows), i32),
        ),
        in_specs=[vmem, vmem],
        out_specs=(vmem, vmem, vmem),
    )(fetch_slab.reshape(2, rows), fetch_row.reshape(2, rows))

    velocity, part0, part1, part2 = pl.pallas_call(
        velocity_kernel,
        name="velocity",
        out_shape=(
            jax.ShapeDtypeStruct((1, rows), f32),
            jax.ShapeDtypeStruct((rows, length), f32),
            jax.ShapeDtypeStruct((rows, length), f32),
            jax.ShapeDtypeStruct((rows, length), f32),
        ),
        in_specs=[smem, smem, smem, vmem, vmem, anywhere, vmem, vmem, vmem, vmem],
        out_specs=(vmem, anywhere, anywhere, anywhere),
        scratch_shapes=[
            pltpu.VMEM((rows, length), f32),
            pltpu.VMEM((rows,) + tile, f32),
            pltpu.VMEM((2, SLABS, 1, LANES), i32),
            pltpu.SMEM((2, SLABS, 1, LANES), i32),
            pltpu.VMEM((2, SLABS, CAP) + tile, f32),
            pltpu.VMEM((SLABS // 2, CAP) + tile, f32),
            pltpu.VMEM((2, SLABS, CAP) + tile, f32),
            pltpu.VMEM((2, SLABS * CAP) + tile, f32),
            pltpu.VMEM((2, SLABS * CAP) + tile, f32),
            pltpu.VMEM((2, SLABS * CAP) + tile, f32),
            pltpu.VMEM((BATCH * CAP,) + tile, f32),
            pltpu.VMEM((BATCH * CAP,) + tile, f32),
            pltpu.VMEM((BATCH * CAP,) + tile, f32),
            pltpu.VMEM((2, SLABS * CAP, LANES), f32),
            pltpu.VMEM((rows, 2 * SLABS * CAP), jnp.bfloat16),
            pltpu.VMEM((3, rows, length), f32),
            pltpu.VMEM((3, 16) + tile, f32),
            pltpu.VMEM((turns, 12, 1, wide), f32),
            pltpu.VMEM((ITERS, SCANS * LAYERS - 1, 1, 2 * LANES), f32),
            pltpu.VMEM((ITERS, 1, 2 * LANES), f32),
            dma, dma((2,)), dma((2,)), dma((2,)), dma((2,)), dma((2, SLABS)),
            dma((SLABS // 2,)), dma,
            dma((turns, 15)), dma((turns, 12)),
            dma((ITERS, SCANS * LAYERS - 1)), dma((ITERS, SCANS * LAYERS - 1)),
            dma((3, 4)),
        ],
        compiler_params=pltpu.CompilerParams(
            collective_id=0, has_side_effects=True, vmem_limit_bytes=56 * MIB
        ),
    )(
        modulus_table, wanting, place, request.reshape(2, SLABS, 1, LANES), place,
        volume.reshape(rows, length), velocity0, modulus_class, high, low,
    )

    block = 128
    across = pl.BlockSpec((1, block), lambda step: (0, step))
    wide_rows = pl.BlockSpec((block, length), lambda step: (step, 0))
    misfit, velocity = pl.pallas_call(
        misfit_kernel,
        name="misfit",
        grid=(rows // block,),
        out_shape=(
            jax.ShapeDtypeStruct((rows, length), f32),
            jax.ShapeDtypeStruct((1, rows), f32),
        ),
        in_specs=[across, wide_rows, wide_rows, wide_rows],
        out_specs=(wide_rows, across),
    )(velocity, part0, part1, part2)
    return velocity, misfit.reshape(volume.shape)


def solution(mesh):
    return jax.shard_map(
        on_device,
        mesh=mesh,
        in_specs=(
            P("scan", "slab", None),
            P("scan", "slab"),
            P("scan", None, "slab", None),
            P("scan", None, "slab"),
            P("scan", "slab"),
            P(),
        ),
        out_specs=(P("scan", "slab"), P("scan", "slab", None)),
        check_vma=False,
    )
```

```python
import math

import jax
import jax.numpy as jnp
import numpy as np
from jax import lax
from jax.experimental import pallas as pl
from jax.experimental.pallas import tpu as pltpu
from jax.sharding import PartitionSpec as P

BAND = 32
ITERS = 2
CAP = 12
LANES = 128
SCANS = 4
SLABS = 64
LAYERS = 8
BATCH = 2
MESH = pl.DeviceIdType.MESH
MIB = 1024 * 1024

root_three = math.sqrt(3.0)
pole_value = math.sqrt(3.0) - 2.0


def filter_parts():
    source = np.arange(LANES)[:, None]
    column = np.arange(2 * LANES)[None, :]
    lane = column % LANES
    beside = np.where(lane < LANES // 2, lane + LANES, lane - LANES)
    distance = np.abs(source - np.where(column < LANES, lane, beside))
    matrix = np.where(distance <= BAND, root_three * pole_value ** distance, 0.0)
    matrix = matrix.astype(np.float32)
    high = matrix.astype(jnp.bfloat16)
    low = (matrix - high.astype(np.float32)).astype(jnp.bfloat16)
    return jnp.asarray(np.concatenate([high, high])), jnp.asarray(low)


def over(number, by):
    return lax.div(number, jnp.int32(by))


def left_of(number, by):
    return lax.rem(number, jnp.int32(by))


def shifts(number):
    phase = left_of(number, 8)
    wave = over(number, 8)
    half = over(phase + 1, 2)
    shift_z = jnp.where(left_of(phase, 2) == 0, left_of(8 - half, 8), half)
    return shift_z, 2 * left_of(wave, 2) + over(wave, 4), left_of(over(wave, 2), 2)


def displaced(slab, number):
    shift_z, shift_x, shift_c = shifts(number)
    core = left_of(left_of(slab, 2) + shift_c, 2)
    at_x = left_of(over(slab, 2) + shift_x, 4)
    at_z = left_of(over(slab, 8) + shift_z, 8)
    return (at_z * 4 + at_x) * 2 + core


def number_between(source, target):
    shift_c = (target % 2 + 2 - source % 2) % 2
    shift_x = ((target // 2) % 4 + 4 - (source // 2) % 4) % 4
    shift_z = (target // 8 + 8 - source // 8) % 8
    phase = jnp.where(shift_z > 4, 2 * (8 - shift_z), jnp.maximum(2 * shift_z - 1, 0))
    wave = shift_x // 2 + 2 * shift_c + 4 * (shift_x % 2)
    return wave * 8 + phase


def velocity_kernel(
    table_ref, peer_ref, row_ref, volume_ref, velocity_ref, class_ref, high_ref, low_ref,
    out_ref, part0_ref, part1_ref, part2_ref,
    volume, by_row, request, wanting, place, asked, asked_scalar, wanting_scalar, place_scalar,
    packed, relay, arrived, value, slope, bend, middle, beside, own, sums, chosen, parts_buf,
    turned, near_box, far_box, totals,
    volume_sem, ask_send, ask_recv, scalar_sem, row_send, row_recv, relay_recv, relay_send,
    near_send, near_recv, far_send, far_recv, part_sem,
):
    scan = lax.axis_index("scan")
    slab = lax.axis_index("slab")
    rows = velocity_ref.shape[1]
    blocks = volume_ref.shape[1] // LANES
    group = SLABS // LAYERS
    position = slab % group
    layer = slab // group
    fars = SCANS * LAYERS
    last = SCANS - 1
    edge = jnp.logical_or(scan == 0, scan == last)
    down = scan >= 1
    up = scan <= last - 1
    present = (up, down)

    volume_copy = pltpu.make_async_copy(volume_ref, volume, volume_sem)
    volume_copy.start()

    barrier = pltpu.get_barrier_semaphore()

    def near_peer(number):
        return (scan, layer * group + left_of(position + 1 + number, group))

    def far_peer(number):
        other = left_of(scan * LAYERS + layer + 1 + number, fars)
        return (over(other, LAYERS), left_of(other, LAYERS) * group + position)

    below = jnp.logical_and(layer >= 1, position <= 1)
    above = layer <= LAYERS - 2
    to_above = jnp.logical_and(above, position >= group - 2)

    def greet(device):
        pl.semaphore_signal(barrier, inc=1, device_id=device, device_id_type=MESH)

    def greet_rows(number, carry):
        @pl.when(down)
        def _():
            greet((scan - 1, number))

        @pl.when(up)
        def _():
            greet((scan + 1, number))

        @pl.when(jnp.logical_and(edge, number != slab))
        def _():
            greet((scan, number))

        return carry

    def greet_far(number, carry):
        greet(far_peer(number))
        return carry

    lax.fori_loop(0, SLABS, greet_rows, 0)
    lax.fori_loop(0, fars - 1, greet_far, 0)
    for number in range(group - 1):
        greet(near_peer(number))

    @pl.when(above)
    def _():
        for number in range(2):
            greet((scan, (layer + 1) * group + number))

    @pl.when(below)
    def _():
        for number in range(group):
            greet((scan, (layer - 1) * group + number))

    expected = (
        jnp.where(edge, 2 * SLABS - 1, 2 * SLABS) + fars - 1 + group - 1
        + jnp.where(above, 2, 0) + jnp.where(below, group, 0)
    )

    earlier = (
        lax.broadcasted_iota(jnp.int32, (rows, rows), 0)
        < lax.broadcasted_iota(jnp.int32, (rows, rows), 1)
    ).astype(jnp.float32).astype(jnp.bfloat16)
    contract = (((1,), (1,)), ((), ()))
    here = lax.broadcasted_iota(jnp.int32, (1, rows), 1)
    for side in range(2):
        peer = peer_ref[side : side + 1, :]
        named = (lax.broadcasted_iota(jnp.int32, (SLABS, rows), 0) == peer).astype(jnp.float32)
        named16 = named.astype(jnp.bfloat16)
        before = jnp.dot(named16, earlier, preferred_element_type=jnp.float32)
        slot = jnp.sum(before * named, axis=0, keepdims=True).astype(jnp.int32)
        at_slot = (lax.broadcasted_iota(jnp.int32, (LANES, rows), 0) == slot).astype(jnp.float32)

        def tabled(numbers):
            high = (at_slot * (numbers // 16).astype(jnp.float32)).astype(jnp.bfloat16)
            low = (at_slot * (numbers % 16).astype(jnp.float32)).astype(jnp.bfloat16)
            table = (
                16.0 * lax.dot_general(named16, high, contract, preferred_element_type=jnp.float32)
                + lax.dot_general(named16, low, contract, preferred_element_type=jnp.float32)
            ).astype(jnp.int32)
            return jnp.clip(table, 0, rows - 1)

        request[side, :, 0, :] = tabled(row_ref[side : side + 1, :])
        wanting[side, :, 0, :] = tabled(here)
        at = number_between(peer, slab) * CAP + jnp.clip(slot, 0, CAP - 1)
        place[side : side + 1, :] = jnp.clip(at, 0, SLABS * CAP - 1)

    volume_copy.wait()

    def relayout(block, carry):
        base = pl.multiple_of(block * 8, 8)
        for part in range(blocks):
            by_row[pl.ds(base, 8), part, :] = volume[
                pl.ds(base, 8), part * LANES : (part + 1) * LANES
            ]
        return carry

    lax.fori_loop(0, rows // 8, relayout, 0)
    pl.semaphore_wait(barrier, expected)

    def ask_copy(side, number):
        return pltpu.make_async_remote_copy(
            src_ref=request.at[side, number],
            dst_ref=asked.at[side, slab],
            send_sem=ask_send.at[side],
            recv_sem=ask_recv.at[side],
            device_id=(scan + 1 - 2 * side, number),
            device_id_type=MESH,
        )

    def ask(number, carry):
        target = left_of(slab + number, SLABS)

        @pl.when(up)
        def _():
            ask_copy(0, target).start()

        @pl.when(down)
        def _():
            ask_copy(1, target).start()

        return carry

    lax.fori_loop(0, SLABS, ask, 0)

    def whole_ask(side):
        return pltpu.make_async_remote_copy(
            src_ref=request.at[side],
            dst_ref=asked.at[side],
            send_sem=ask_send.at[side],
            recv_sem=ask_recv.at[side],
            device_id=(scan, slab),
            device_id_type=MESH,
        )

    def near_copy(turn, index, entry, device):
        return pltpu.make_async_remote_copy(
            src_ref=near_box.at[turn, position + 2],
            dst_ref=near_box.at[turn, entry],
            send_sem=near_send.at[turn, index],
            recv_sem=near_recv.at[turn, entry],
            device_id=device,
            device_id_type=MESH,
        )

    def shares(turn, act):
        for number in range(group - 1):
            act(near_copy(turn, number, position + 2, near_peer(number)))

        @pl.when(below)
        def _():
            for number in range(group):
                act(near_copy(turn, 7 + number, position + group + 2, (scan, (layer - 1) * group + number)))

        @pl.when(to_above)
        def _():
            for number in range(2):
                act(near_copy(turn, 7 + number, position - group + 2, (scan, (layer + 1) * group + number)))

    def share(turn, message):
        near_box[turn, position + 2] = message
        shares(turn, lambda copy: copy.start())

    def collect(turn):
        def wait(entry):
            near_copy(turn, 0, entry, (scan, slab)).wait_recv()

        for entry in range(2, group + 2):
            @pl.when(position + 2 != entry)
            def _():
                wait(entry)

        @pl.when(above)
        def _():
            wait(group + 2)
            wait(group + 3)

        @pl.when(below)
        def _():
            wait(0)
            wait(1)

        shares(turn, lambda copy: copy.wait_send())

    lane_row = lax.broadcasted_iota(jnp.int32, (1, rows), 1)

    def stencil(turn, field):
        def entry(offset):
            return near_box[turn, position + 2 + offset, :, :rows]

        lower1 = jnp.where(slab >= 1, entry(-1), 0.0)
        lower2 = jnp.where(slab >= 2, entry(-2), 0.0)
        upper1 = jnp.where(slab <= SLABS - 2, entry(1), 0.0)
        upper2 = jnp.where(slab <= SLABS - 3, entry(2), 0.0)
        left = jnp.where(lane_row == 0, pltpu.roll(lower1, 1, 1), pltpu.roll(field, 1, 1))
        right = jnp.where(
            lane_row == rows - 1, pltpu.roll(upper1, rows - 1, 1), pltpu.roll(field, rows - 1, 1)
        )
        return 4.0 * field - left - right - lower2 - upper2

    weight = jnp.zeros((1, rows), jnp.float32)
    for number in range(4):
        weight = jnp.where(class_ref[...] == number, table_ref[number], weight)
    stiffness = jnp.sqrt(weight)
    velocity = velocity_ref[...]

    wanting_copy = pltpu.make_async_copy(wanting, wanting_scalar, scalar_sem.at[2])
    place_copy = pltpu.make_async_copy(place, place_scalar, scalar_sem.at[3])
    wanting_copy.start()
    place_copy.start()

    def scalar_copy(side):
        return pltpu.make_async_copy(asked.at[side], asked_scalar.at[side], scalar_sem.at[side])

    for side, serving in ((0, down), (1, up)):
        @pl.when(serving)
        def _():
            whole_ask(side).wait_recv()
            scalar_copy(side).start()

    for side, serving in ((0, down), (1, up)):
        @pl.when(serving)
        def _():
            scalar_copy(side).wait()

    def row_copy(source, side, number, target, target_scan, send_sem):
        return pltpu.make_async_remote_copy(
            src_ref=source,
            dst_ref=arrived.at[side, number],
            send_sem=send_sem,
            recv_sem=row_recv.at[side, number],
            device_id=(target_scan, target),
            device_id_type=MESH,
        )

    def relay_copy(side, number, relay_number, target_scan):
        return pltpu.make_async_remote_copy(
            src_ref=packed.at[side, number],
            dst_ref=relay.at[relay_number],
            send_sem=row_send.at[side],
            recv_sem=relay_recv.at[relay_number],
            device_id=(target_scan, slab),
            device_id_type=MESH,
        )

    def serve(side, number, target, relayed_scan):
        target_scan = scan - 1 + 2 * side
        relay_number = (number // 16) * 8 + number % 8
        relayed = jnp.logical_and(scan == relayed_scan, (number // 8) % 2 == 1)
        for slot in range(CAP):
            packed[side, number, slot] = by_row[asked_scalar[side, target, 0, slot]]

        @pl.when(relayed)
        def _():
            relay_copy(side, number, relay_number, target_scan).start()

        @pl.when(jnp.logical_not(relayed))
        def _():
            row_copy(
                packed.at[side, number], side, number, target, target_scan, row_send.at[side]
            ).start()

    def send(number, carry):
        target = displaced(slab, number)

        @pl.when(down)
        def _():
            serve(0, number, target, 1)

        @pl.when(up)
        def _():
            serve(1, number, target, 2)

        return carry

    lax.fori_loop(0, SLABS, send, 0)
    blank = jnp.zeros((1, 2 * LANES), jnp.float32)
    share(0, jnp.concatenate([stiffness * velocity, blank], axis=1))

    wanting_copy.wait()
    place_copy.wait()
    for side in range(2):
        across = place[side : side + 1, :].astype(jnp.float32)
        upright = jnp.transpose(jnp.broadcast_to(across, (LANES, rows)))
        lane = lax.broadcasted_iota(jnp.int32, (rows, LANES), 1).astype(jnp.float32)
        for block in range(SLABS * CAP // LANES):
            at = side * SLABS * CAP + block * LANES
            chosen[:, at : at + LANES] = (
                (upright == lane + float(block * LANES)).astype(jnp.float32).astype(jnp.bfloat16)
            )

        @pl.when(jnp.logical_not(present[side]))
        def _():
            sums[side] = jnp.zeros(sums.shape[1:], jnp.float32)

    lane8 = lax.broadcasted_iota(jnp.int32, (8, LANES), 1)
    zero8 = jnp.zeros((8, LANES), jnp.float32)
    batch_rows = BATCH * CAP

    def absorb(side, batch):
        for one in range(BATCH):
            number = batch * BATCH + one
            row_copy(packed.at[side, number], side, number, slab, scan, row_send.at[side]).wait_recv()
        voxels = arrived[side, pl.ds(batch * BATCH, BATCH)].reshape(batch_rows * blocks, LANES)
        top = voxels.astype(jnp.bfloat16)
        rest = (voxels - top.astype(jnp.float32)).astype(jnp.bfloat16)
        both = jnp.dot(
            jnp.concatenate([top, rest], axis=1), high_ref[...], preferred_element_type=jnp.float32
        ) + jnp.dot(top, low_ref[...], preferred_element_type=jnp.float32)
        middle[...] = both[:, :LANES].reshape(batch_rows, blocks, LANES)
        beside[...] = both[:, LANES:].reshape(batch_rows, blocks, LANES)
        for chunk in range(BATCH):
            source = displaced_back(batch * BATCH + chunk)
            for slot in range(CAP):
                own[chunk * CAP + slot] = by_row[wanting_scalar[side, source, 0, slot]]

        def combine(eight, carry):
            at = pl.ds(pl.multiple_of(eight * 8, 8), 8)
            to = pl.ds(pl.multiple_of(batch * batch_rows + eight * 8, 8), 8)
            coeffs = []
            for block in range(blocks):
                left = beside[at, block - 1, :] if block > 0 else zero8
                right = beside[at, block + 1, :] if block < blocks - 1 else zero8
                coeffs.append(middle[at, block, :] + jnp.where(lane8 < LANES // 2, left, right))
            to_right = [pltpu.roll(one, 1, 1) for one in coeffs]
            to_left = [pltpu.roll(one, LANES - 1, 1) for one in coeffs]
            total = [zero8] * 5
            for block in range(blocks):
                prior = jnp.where(lane8 == 0, to_right[block - 1] if block > 0 else zero8, to_right[block])
                after = jnp.where(
                    lane8 == LANES - 1,
                    to_left[block + 1] if block < blocks - 1 else zero8,
                    to_left[block],
                )
                ends = prior + after
                v = (ends + 4.0 * coeffs[block]) * (1.0 / 6.0)
                s = 0.5 * (after - prior)
                b = ends - 2.0 * coeffs[block]
                off = v - own[at, block, :]
                value[side, to, block, :] = v
                slope[side, to, block, :] = s
                bend[side, to, block, :] = b
                total[0] += s * off
                total[1] += b * off
                total[2] += s * s
                total[3] += s * b
                total[4] += b * b
            column = zero8
            for number in range(5):
                summed = jnp.sum(total[number], axis=1, keepdims=True)
                if side == 1 and number in (0, 3):
                    summed = -summed
                column = jnp.where(lane8 % 8 == number, summed, column)
            first = column.astype(jnp.bfloat16).astype(jnp.float32)
            second = (column - first).astype(jnp.bfloat16).astype(jnp.float32)
            third = (column - first - second).astype(jnp.bfloat16).astype(jnp.float32)
            column = jnp.where(lane8 < 8, first, jnp.where(lane8 < 16, second, third))
            sums[side, to, :] = jnp.where(lane8 < 24, column, 0.0)
            return carry

        lax.fori_loop(0, batch_rows // 8, combine, 0)

    def displaced_back(number):
        shift_z, shift_x, shift_c = shifts(number)
        core = left_of(left_of(slab, 2) + 2 - shift_c, 2)
        at_x = left_of(over(slab, 2) + 4 - shift_x, 4)
        at_z = left_of(over(slab, 8) + 8 - shift_z, 8)
        return (at_z * 4 + at_x) * 2 + core

    def pass_on(side, relay_number):
        number = (relay_number // 8) * 16 + 8 + relay_number % 8
        relay_copy(side, number, relay_number, scan).wait_recv()
        row_copy(
            relay.at[relay_number], side, number, displaced(slab, number), scan, relay_send
        ).start()

    def step(batch, carry):
        for side, relaying in ((0, scan == 0), (1, scan == last)):
            @pl.when(jnp.logical_and(relaying, batch < SLABS // 8))
            def _():
                for one in range(4):
                    pass_on(side, batch * 4 + one)

        for side in range(2):
            @pl.when(present[side])
            def _():
                absorb(side, batch)

        return carry

    lax.fori_loop(0, SLABS // BATCH, step, 0)

    collect(0)
    smooth = stencil(0, stiffness * velocity)
    moments = jnp.dot(
        chosen[...],
        sums[...].reshape(2 * SLABS * CAP, LANES).astype(jnp.bfloat16),
        preferred_element_type=jnp.float32,
    )
    moments = jnp.transpose(moments)
    moments = moments[0:8] + moments[8:16] + moments[16:24]
    m0, m1, m2, m3, m4 = (moments[number : number + 1, :] for number in range(5))

    def coefficients(quarter):
        def one_row(row, at):
            forward = place_scalar[0, row]
            backward = place_scalar[1, row]

            def got(ref):
                return (
                    jnp.where(up, ref[0, forward], 0.0),
                    jnp.where(down, ref[1, backward], 0.0),
                )

            value_f, value_b = got(value)
            slope_f, slope_b = got(slope)
            bend_f, bend_b = got(bend)
            turned[0, at] = value_f + value_b - 2.0 * by_row[row]
            turned[1, at] = slope_f - slope_b
            turned[2, at] = 0.5 * (bend_f + bend_b)

        def eight(step, carry):
            base = pl.multiple_of(quarter * (rows // 4) + step * 8, 8)
            half = (step % 2) * 8
            for one in range(8):
                one_row(base + one, half + one)
            for number in range(3):
                for block in range(blocks):
                    parts_buf[number, pl.ds(base, 8), block * LANES : (block + 1) * LANES] = turned[
                        number, pl.ds(pl.multiple_of(half, 8), 8), block, :
                    ]
            return carry

        lax.fori_loop(0, rows // 32, eight, 0)
        for copy in part_copies(quarter):
            copy.start()

    def part_copies(quarter):
        at = pl.ds(quarter * (rows // 4), rows // 4)
        return [
            pltpu.make_async_copy(parts_buf.at[number, at], ref.at[at], part_sem.at[number, quarter])
            for number, ref in enumerate((part0_ref, part1_ref, part2_ref))
        ]

    def folded(values):
        return sum(values[:, at : at + LANES] for at in range(0, rows, LANES))

    for turn in range(ITERS):
        linear = m0 + velocity * (m1 + m2) + 1.5 * velocity * velocity * m3 + (
            0.5 * velocity * velocity * velocity * m4
        )
        curvature = m2 + 2.0 * velocity * m3 + velocity * velocity * m4
        gradient = linear + stiffness * smooth
        direction = gradient / (curvature + 4.0 * stiffness * stiffness)
        scaled = stiffness * direction
        share(
            turn + 1,
            jnp.concatenate(
                [
                    scaled,
                    folded(direction * gradient),
                    folded(curvature * direction * direction + 4.0 * scaled * scaled),
                ],
                axis=1,
            ),
        )
        coefficients(2 * turn)
        collect(turn + 1)
        box = near_box[turn + 1, :, 0, :]
        fields = box[2 : group + 2, :rows]
        beyond = jnp.where(
            jnp.logical_or(above, lax.broadcasted_iota(jnp.int32, (4, rows), 0) < 2),
            box[group : group + 4, :rows], 0.0,
        )
        next1 = jnp.concatenate([box[3 : group + 2, :rows], beyond[2:3]], axis=0)
        next2 = jnp.concatenate([box[4 : group + 2, :rows], beyond[2:4]], axis=0)
        lane_all = lax.broadcasted_iota(jnp.int32, (group, rows), 1)
        right = jnp.where(
            lane_all == rows - 1, pltpu.roll(next1, rows - 1, 1), pltpu.roll(fields, rows - 1, 1)
        )
        cross = jnp.sum(folded(fields * (right + next2)), axis=0, keepdims=True)
        mine = jnp.sum(box[2 : group + 2, rows:], axis=0, keepdims=True)
        mine = mine - jnp.concatenate([jnp.zeros_like(cross), 2.0 * cross], axis=1)
        totals[turn] = mine

        def far_copy(number):
            return pltpu.make_async_remote_copy(
                src_ref=totals.at[turn],
                dst_ref=far_box.at[turn, number],
                send_sem=far_send.at[turn, number],
                recv_sem=far_recv.at[turn, number],
                device_id=far_peer(number),
                device_id_type=MESH,
            )

        def far_start(number, carry):
            far_copy(number).start()
            return carry

        def far_wait(number, carry):
            far_copy(number).wait()
            return carry

        lax.fori_loop(0, fars - 1, far_start, 0)
        bent = stencil(turn + 1, scaled)
        coefficients(2 * turn + 1)
        lax.fori_loop(0, fars - 1, far_wait, 0)
        mine = mine + jnp.sum(far_box[turn], axis=0)
        upper = jnp.sum(mine[:, :LANES], axis=1, keepdims=True)
        lower = jnp.sum(mine[:, LANES:], axis=1, keepdims=True)
        alpha = upper / lower
        velocity = velocity - alpha * direction
        smooth = smooth - alpha * bent
    out_ref[...] = velocity

    @pl.when(up)
    def _():
        whole_ask(0).wait_send()

    @pl.when(down)
    def _():
        whole_ask(1).wait_send()

    for side, serving in ((0, down), (1, up)):
        @pl.when(serving)
        def _():
            pltpu.make_async_remote_copy(
                src_ref=packed.at[side],
                dst_ref=arrived.at[side],
                send_sem=row_send.at[side],
                recv_sem=row_recv.at[side, 0],
                device_id=(scan, slab),
                device_id_type=MESH,
            ).wait_send()

    @pl.when(edge)
    def _():
        pltpu.make_async_remote_copy(
            src_ref=relay,
            dst_ref=relay,
            send_sem=relay_send,
            recv_sem=relay_recv.at[0],
            device_id=(scan, slab),
            device_id_type=MESH,
        ).wait_send()

    for quarter in range(4):
        for copy in part_copies(quarter):
            copy.wait()


def misfit_kernel(velocity_ref, part0_ref, part1_ref, part2_ref, out_ref, velocity_out_ref):
    rows = out_ref.shape[0]
    across = velocity_ref[...]
    velocity_out_ref[...] = across
    moved = jnp.transpose(jnp.broadcast_to(across, (rows, rows)))
    for at in range(0, out_ref.shape[1], LANES):
        columns = slice(at, at + LANES)
        out_ref[:, columns] = part0_ref[:, columns] + moved * (
            part1_ref[:, columns] + moved * part2_ref[:, columns]
        )


def on_device(volume, velocity0, fetch_slab, fetch_row, modulus_class, modulus_table):
    rows, length = volume.shape[1:]
    blocks = length // LANES
    f32 = jnp.float32
    i32 = jnp.int32
    vmem = pl.BlockSpec(memory_space=pltpu.VMEM)
    smem = pl.BlockSpec(memory_space=pltpu.SMEM)
    anywhere = pl.BlockSpec(memory_space=pl.ANY)
    dma = pltpu.SemaphoreType.DMA
    high, low = filter_parts()
    tile = (blocks, LANES)
    turns = ITERS + 1
    wide = rows + 2 * LANES

    velocity, part0, part1, part2 = pl.pallas_call(
        velocity_kernel,
        name="velocity",
        out_shape=(
            jax.ShapeDtypeStruct((1, rows), f32),
            jax.ShapeDtypeStruct((rows, length), f32),
            jax.ShapeDtypeStruct((rows, length), f32),
            jax.ShapeDtypeStruct((rows, length), f32),
        ),
        in_specs=[smem, vmem, vmem, anywhere, vmem, vmem, vmem, vmem],
        out_specs=(vmem, anywhere, anywhere, anywhere),
        scratch_shapes=[
            pltpu.VMEM((rows, length), f32),
            pltpu.VMEM((rows,) + tile, f32),
            pltpu.VMEM((2, SLABS, 1, LANES), i32),
            pltpu.VMEM((2, SLABS, 1, LANES), i32),
            pltpu.VMEM((2, rows), i32),
            pltpu.VMEM((2, SLABS, 1, LANES), i32),
            pltpu.SMEM((2, SLABS, 1, LANES), i32),
            pltpu.SMEM((2, SLABS, 1, LANES), i32),
            pltpu.SMEM((2, rows), i32),
            pltpu.VMEM((2, SLABS, CAP) + tile, f32),
            pltpu.VMEM((SLABS // 2, CAP) + tile, f32),
            pltpu.VMEM((2, SLABS, CAP) + tile, f32),
            pltpu.VMEM((2, SLABS * CAP) + tile, f32),
            pltpu.VMEM((2, SLABS * CAP) + tile, f32),
            pltpu.VMEM((2, SLABS * CAP) + tile, f32),
            pltpu.VMEM((BATCH * CAP,) + tile, f32),
            pltpu.VMEM((BATCH * CAP,) + tile, f32),
            pltpu.VMEM((BATCH * CAP,) + tile, f32),
            pltpu.VMEM((2, SLABS * CAP, LANES), f32),
            pltpu.VMEM((rows, 2 * SLABS * CAP), jnp.bfloat16),
            pltpu.VMEM((3, rows, length), f32),
            pltpu.VMEM((3, 16) + tile, f32),
            pltpu.VMEM((turns, 12, 1, wide), f32),
            pltpu.VMEM((ITERS, SCANS * LAYERS - 1, 1, 2 * LANES), f32),
            pltpu.VMEM((ITERS, 1, 2 * LANES), f32),
            dma, dma((2,)), dma((2,)), dma((4,)), dma((2,)), dma((2, SLABS)),
            dma((SLABS // 2,)), dma,
            dma((turns, 15)), dma((turns, 12)),
            dma((ITERS, SCANS * LAYERS - 1)), dma((ITERS, SCANS * LAYERS - 1)),
            dma((3, 4)),
        ],
        compiler_params=pltpu.CompilerParams(
            collective_id=0, has_side_effects=True, vmem_limit_bytes=56 * MIB
        ),
    )(
        modulus_table, fetch_slab.reshape(2, rows), fetch_row.reshape(2, rows),
        volume.reshape(rows, length), velocity0, modulus_class, high, low,
    )

    block = 128
    across = pl.BlockSpec((1, block), lambda step: (0, step))
    wide_rows = pl.BlockSpec((block, length), lambda step: (step, 0))
    misfit, velocity = pl.pallas_call(
        misfit_kernel,
        name="misfit",
        grid=(rows // block,),
        out_shape=(
            jax.ShapeDtypeStruct((rows, length), f32),
            jax.ShapeDtypeStruct((1, rows), f32),
        ),
        in_specs=[across, wide_rows, wide_rows, wide_rows],
        out_specs=(wide_rows, across),
    )(velocity, part0, part1, part2)
    return velocity, misfit.reshape(volume.shape)


def solution(mesh):
    return jax.shard_map(
        on_device,
        mesh=mesh,
        in_specs=(
            P("scan", "slab", None),
            P("scan", "slab"),
            P("scan", None, "slab", None),
            P("scan", None, "slab"),
            P("scan", "slab"),
            P(),
        ),
        out_specs=(P("scan", "slab"), P("scan", "slab", None)),
        check_vma=False,
    )
```

```python
import math

import jax
import jax.numpy as jnp
import numpy as np
from jax import lax
from jax.experimental import pallas as pl
from jax.experimental.pallas import tpu as pltpu
from jax.sharding import PartitionSpec as P

BAND = 32
ITERS = 2
CAP = 12
LANES = 128
SCANS = 4
SLABS = 64
LAYERS = 8
BATCH = 2
MESH = pl.DeviceIdType.MESH
MIB = 1024 * 1024

root_three = math.sqrt(3.0)
pole_value = math.sqrt(3.0) - 2.0


def filter_parts():
    source = np.arange(LANES)[:, None]
    column = np.arange(2 * LANES)[None, :]
    lane = column % LANES
    beside = np.where(lane < LANES // 2, lane + LANES, lane - LANES)
    distance = np.abs(source - np.where(column < LANES, lane, beside))
    matrix = np.where(distance <= BAND, root_three * pole_value ** distance, 0.0)
    matrix = matrix.astype(np.float32)
    high = matrix.astype(jnp.bfloat16)
    low = (matrix - high.astype(np.float32)).astype(jnp.bfloat16)
    return jnp.asarray(np.concatenate([high, high])), jnp.asarray(low)


def over(number, by):
    return lax.div(number, jnp.int32(by))


def left_of(number, by):
    return lax.rem(number, jnp.int32(by))


def shifts(number):
    phase = left_of(number, 8)
    wave = over(number, 8)
    half = over(phase + 1, 2)
    shift_z = jnp.where(left_of(phase, 2) == 0, left_of(8 - half, 8), half)
    return shift_z, 2 * left_of(wave, 2) + over(wave, 4), left_of(over(wave, 2), 2)


def displaced(slab, number):
    shift_z, shift_x, shift_c = shifts(number)
    core = left_of(left_of(slab, 2) + shift_c, 2)
    at_x = left_of(over(slab, 2) + shift_x, 4)
    at_z = left_of(over(slab, 8) + shift_z, 8)
    return (at_z * 4 + at_x) * 2 + core


def number_between(source, target):
    shift_c = (target % 2 + 2 - source % 2) % 2
    shift_x = ((target // 2) % 4 + 4 - (source // 2) % 4) % 4
    shift_z = (target // 8 + 8 - source // 8) % 8
    phase = jnp.where(shift_z > 4, 2 * (8 - shift_z), jnp.maximum(2 * shift_z - 1, 0))
    wave = shift_x // 2 + 2 * shift_c + 4 * (shift_x % 2)
    return wave * 8 + phase


def velocity_kernel(
    table_ref, peer_ref, row_ref, volume_ref, velocity_ref, class_ref, high_ref, low_ref,
    out_ref, part0_ref, part1_ref, part2_ref,
    volume, by_row, request, wanting, place, asked, asked_scalar, wanting_scalar, place_scalar,
    packed, relay, arrived, value, slope, bend, middle, beside, own, sums, chosen, parts_buf,
    turned, near_box, far_box, totals,
    volume_sem, ask_send, ask_recv, scalar_sem, row_send, row_recv, relay_recv, relay_send,
    near_send, near_recv, far_send, far_recv, part_sem,
):
    scan = lax.axis_index("scan")
    slab = lax.axis_index("slab")
    rows = velocity_ref.shape[1]
    blocks = volume_ref.shape[1] // LANES
    group = SLABS // LAYERS
    position = slab % group
    layer = slab // group
    fars = SCANS * LAYERS
    last = SCANS - 1
    edge = jnp.logical_or(scan == 0, scan == last)
    down = scan >= 1
    up = scan <= last - 1
    present = (up, down)

    volume_copy = pltpu.make_async_copy(volume_ref, volume, volume_sem)
    volume_copy.start()

    barrier = pltpu.get_barrier_semaphore()

    def near_peer(number):
        return (scan, layer * group + left_of(position + 1 + number, group))

    def far_peer(number):
        other = left_of(scan * LAYERS + layer + 1 + number, fars)
        return (over(other, LAYERS), left_of(other, LAYERS) * group + position)

    below = jnp.logical_and(layer >= 1, position <= 1)
    above = layer <= LAYERS - 2
    to_above = jnp.logical_and(above, position >= group - 2)

    def greet(device):
        pl.semaphore_signal(barrier, inc=1, device_id=device, device_id_type=MESH)

    def greet_rows(number, carry):
        @pl.when(down)
        def _():
            greet((scan - 1, number))

        @pl.when(up)
        def _():
            greet((scan + 1, number))

        return carry

    lax.fori_loop(0, SLABS, greet_rows, 0)
    expected = jnp.where(edge, SLABS, 2 * SLABS)

    earlier = (
        lax.broadcasted_iota(jnp.int32, (rows, rows), 0)
        < lax.broadcasted_iota(jnp.int32, (rows, rows), 1)
    ).astype(jnp.float32).astype(jnp.bfloat16)
    contract = (((1,), (1,)), ((), ()))
    here = lax.broadcasted_iota(jnp.int32, (1, rows), 1)
    for side in range(2):
        peer = peer_ref[side : side + 1, :]
        named = (lax.broadcasted_iota(jnp.int32, (SLABS, rows), 0) == peer).astype(jnp.float32)
        named16 = named.astype(jnp.bfloat16)
        before = jnp.dot(named16, earlier, preferred_element_type=jnp.float32)
        slot = jnp.sum(before * named, axis=0, keepdims=True).astype(jnp.int32)
        at_slot = (lax.broadcasted_iota(jnp.int32, (LANES, rows), 0) == slot).astype(jnp.float32)

        def tabled(numbers):
            high = (at_slot * (numbers // 16).astype(jnp.float32)).astype(jnp.bfloat16)
            low = (at_slot * (numbers % 16).astype(jnp.float32)).astype(jnp.bfloat16)
            table = (
                16.0 * lax.dot_general(named16, high, contract, preferred_element_type=jnp.float32)
                + lax.dot_general(named16, low, contract, preferred_element_type=jnp.float32)
            ).astype(jnp.int32)
            return jnp.clip(table, 0, rows - 1)

        request[side, :, 0, :] = tabled(row_ref[side : side + 1, :])
        wanting[side, :, 0, :] = tabled(here)
        at = number_between(peer, slab) * CAP + jnp.clip(slot, 0, CAP - 1)
        place[side : side + 1, :] = jnp.clip(at, 0, SLABS * CAP - 1)

    volume_copy.wait()

    def relayout(block, carry):
        base = pl.multiple_of(block * 8, 8)
        for part in range(blocks):
            by_row[pl.ds(base, 8), part, :] = volume[
                pl.ds(base, 8), part * LANES : (part + 1) * LANES
            ]
        return carry

    lax.fori_loop(0, rows // 8, relayout, 0)
    pl.semaphore_wait(barrier, expected)

    def ask_copy(side, number):
        return pltpu.make_async_remote_copy(
            src_ref=request.at[side, number],
            dst_ref=asked.at[side, slab],
            send_sem=ask_send.at[side],
            recv_sem=ask_recv.at[side],
            device_id=(scan + 1 - 2 * side, number),
            device_id_type=MESH,
        )

    def ask(number, carry):
        target = left_of(slab + number, SLABS)

        @pl.when(up)
        def _():
            ask_copy(0, target).start()

        @pl.when(down)
        def _():
            ask_copy(1, target).start()

        return carry

    lax.fori_loop(0, SLABS, ask, 0)

    def whole_ask(side):
        return pltpu.make_async_remote_copy(
            src_ref=request.at[side],
            dst_ref=asked.at[side],
            send_sem=ask_send.at[side],
            recv_sem=ask_recv.at[side],
            device_id=(scan, slab),
            device_id_type=MESH,
        )

    def near_copy(turn, index, entry, device):
        return pltpu.make_async_remote_copy(
            src_ref=near_box.at[turn, position + 2],
            dst_ref=near_box.at[turn, entry],
            send_sem=near_send.at[turn, index],
            recv_sem=near_recv.at[turn, entry],
            device_id=device,
            device_id_type=MESH,
        )

    def shares(turn, act):
        for number in range(group - 1):
            act(near_copy(turn, number, position + 2, near_peer(number)))

        @pl.when(below)
        def _():
            for number in range(group):
                act(near_copy(turn, 7 + number, position + group + 2, (scan, (layer - 1) * group + number)))

        @pl.when(to_above)
        def _():
            for number in range(2):
                act(near_copy(turn, 7 + number, position - group + 2, (scan, (layer + 1) * group + number)))

    def share(turn, message):
        near_box[turn, position + 2] = message
        shares(turn, lambda copy: copy.start())

    def collect(turn):
        def wait(entry):
            near_copy(turn, 0, entry, (scan, slab)).wait_recv()

        for entry in range(2, group + 2):
            @pl.when(position + 2 != entry)
            def _():
                wait(entry)

        @pl.when(above)
        def _():
            wait(group + 2)
            wait(group + 3)

        @pl.when(below)
        def _():
            wait(0)
            wait(1)

    lane_row = lax.broadcasted_iota(jnp.int32, (1, rows), 1)

    def stencil(turn, field):
        def entry(offset):
            return near_box[turn, position + 2 + offset, :, :rows]

        lower1 = jnp.where(slab >= 1, entry(-1), 0.0)
        lower2 = jnp.where(slab >= 2, entry(-2), 0.0)
        upper1 = jnp.where(slab <= SLABS - 2, entry(1), 0.0)
        upper2 = jnp.where(slab <= SLABS - 3, entry(2), 0.0)
        left = jnp.where(lane_row == 0, pltpu.roll(lower1, 1, 1), pltpu.roll(field, 1, 1))
        right = jnp.where(
            lane_row == rows - 1, pltpu.roll(upper1, rows - 1, 1), pltpu.roll(field, rows - 1, 1)
        )
        return 4.0 * field - left - right - lower2 - upper2

    weight = jnp.zeros((1, rows), jnp.float32)
    for number in range(4):
        weight = jnp.where(class_ref[...] == number, table_ref[number], weight)
    stiffness = jnp.sqrt(weight)
    velocity = velocity_ref[...]

    wanting_copy = pltpu.make_async_copy(wanting, wanting_scalar, scalar_sem.at[2])
    place_copy = pltpu.make_async_copy(place, place_scalar, scalar_sem.at[3])
    wanting_copy.start()
    place_copy.start()

    def scalar_copy(side):
        return pltpu.make_async_copy(asked.at[side], asked_scalar.at[side], scalar_sem.at[side])

    for side, serving in ((0, down), (1, up)):
        @pl.when(serving)
        def _():
            whole_ask(side).wait_recv()
            scalar_copy(side).start()

    for side, serving in ((0, down), (1, up)):
        @pl.when(serving)
        def _():
            scalar_copy(side).wait()

    def row_copy(source, side, number, target, target_scan, send_sem):
        return pltpu.make_async_remote_copy(
            src_ref=source,
            dst_ref=arrived.at[side, number],
            send_sem=send_sem,
            recv_sem=row_recv.at[side, number],
            device_id=(target_scan, target),
            device_id_type=MESH,
        )

    def relay_copy(side, number, relay_number, target_scan):
        return pltpu.make_async_remote_copy(
            src_ref=packed.at[side, number],
            dst_ref=relay.at[relay_number],
            send_sem=row_send.at[side],
            recv_sem=relay_recv.at[relay_number],
            device_id=(target_scan, slab),
            device_id_type=MESH,
        )

    def serve(side, number, target, relayed_scan):
        target_scan = scan - 1 + 2 * side
        relay_number = (number // 16) * 8 + number % 8
        relayed = jnp.logical_and(scan == relayed_scan, (number // 8) % 2 == 1)
        for slot in range(CAP):
            packed[side, number, slot] = by_row[asked_scalar[side, target, 0, slot]]

        @pl.when(relayed)
        def _():
            relay_copy(side, number, relay_number, target_scan).start()

        @pl.when(jnp.logical_not(relayed))
        def _():
            row_copy(
                packed.at[side, number], side, number, target, target_scan, row_send.at[side]
            ).start()

    def send(number, carry):
        target = displaced(slab, number)

        @pl.when(down)
        def _():
            serve(0, number, target, 1)

        @pl.when(up)
        def _():
            serve(1, number, target, 2)

        return carry

    lax.fori_loop(0, SLABS, send, 0)
    blank = jnp.zeros((1, 2 * LANES), jnp.float32)
    share(0, jnp.concatenate([stiffness * velocity, blank], axis=1))

    wanting_copy.wait()
    place_copy.wait()
    for side in range(2):
        across = place[side : side + 1, :].astype(jnp.float32)
        upright = jnp.transpose(jnp.broadcast_to(across, (LANES, rows)))
        lane = lax.broadcasted_iota(jnp.int32, (rows, LANES), 1).astype(jnp.float32)
        for block in range(SLABS * CAP // LANES):
            at = side * SLABS * CAP + block * LANES
            chosen[:, at : at + LANES] = (
                (upright == lane + float(block * LANES)).astype(jnp.float32).astype(jnp.bfloat16)
            )

        @pl.when(jnp.logical_not(present[side]))
        def _():
            sums[side] = jnp.zeros(sums.shape[1:], jnp.float32)

    lane8 = lax.broadcasted_iota(jnp.int32, (8, LANES), 1)
    zero8 = jnp.zeros((8, LANES), jnp.float32)
    batch_rows = BATCH * CAP

    def absorb(side, batch):
        for one in range(BATCH):
            number = batch * BATCH + one
            row_copy(packed.at[side, number], side, number, slab, scan, row_send.at[side]).wait_recv()
        voxels = arrived[side, pl.ds(batch * BATCH, BATCH)].reshape(batch_rows * blocks, LANES)
        top = voxels.astype(jnp.bfloat16)
        rest = (voxels - top.astype(jnp.float32)).astype(jnp.bfloat16)
        both = jnp.dot(
            jnp.concatenate([top, rest], axis=1), high_ref[...], preferred_element_type=jnp.float32
        ) + jnp.dot(top, low_ref[...], preferred_element_type=jnp.float32)
        middle[...] = both[:, :LANES].reshape(batch_rows, blocks, LANES)
        beside[...] = both[:, LANES:].reshape(batch_rows, blocks, LANES)
        for chunk in range(BATCH):
            source = displaced_back(batch * BATCH + chunk)
            for slot in range(CAP):
                own[chunk * CAP + slot] = by_row[wanting_scalar[side, source, 0, slot]]

        def combine(eight, carry):
            at = pl.ds(pl.multiple_of(eight * 8, 8), 8)
            to = pl.ds(pl.multiple_of(batch * batch_rows + eight * 8, 8), 8)
            coeffs = []
            for block in range(blocks):
                left = beside[at, block - 1, :] if block > 0 else zero8
                right = beside[at, block + 1, :] if block < blocks - 1 else zero8
                coeffs.append(middle[at, block, :] + jnp.where(lane8 < LANES // 2, left, right))
            to_right = [pltpu.roll(one, 1, 1) for one in coeffs]
            to_left = [pltpu.roll(one, LANES - 1, 1) for one in coeffs]
            total = [zero8] * 5
            for block in range(blocks):
                prior = jnp.where(lane8 == 0, to_right[block - 1] if block > 0 else zero8, to_right[block])
                after = jnp.where(
                    lane8 == LANES - 1,
                    to_left[block + 1] if block < blocks - 1 else zero8,
                    to_left[block],
                )
                ends = prior + after
                v = (ends + 4.0 * coeffs[block]) * (1.0 / 6.0)
                s = 0.5 * (after - prior)
                b = ends - 2.0 * coeffs[block]
                off = v - own[at, block, :]
                value[side, to, block, :] = v
                slope[side, to, block, :] = s
                bend[side, to, block, :] = b
                total[0] += s * off
                total[1] += b * off
                total[2] += s * s
                total[3] += s * b
                total[4] += b * b
            column = zero8
            for number in range(5):
                summed = jnp.sum(total[number], axis=1, keepdims=True)
                if side == 1 and number in (0, 3):
                    summed = -summed
                column = jnp.where(lane8 % 8 == number, summed, column)
            first = column.astype(jnp.bfloat16).astype(jnp.float32)
            second = (column - first).astype(jnp.bfloat16).astype(jnp.float32)
            third = (column - first - second).astype(jnp.bfloat16).astype(jnp.float32)
            column = jnp.where(lane8 < 8, first, jnp.where(lane8 < 16, second, third))
            sums[side, to, :] = jnp.where(lane8 < 24, column, 0.0)
            return carry

        lax.fori_loop(0, batch_rows // 8, combine, 0)

    def displaced_back(number):
        shift_z, shift_x, shift_c = shifts(number)
        core = left_of(left_of(slab, 2) + 2 - shift_c, 2)
        at_x = left_of(over(slab, 2) + 4 - shift_x, 4)
        at_z = left_of(over(slab, 8) + 8 - shift_z, 8)
        return (at_z * 4 + at_x) * 2 + core

    def pass_on(side, relay_number):
        number = (relay_number // 8) * 16 + 8 + relay_number % 8
        relay_copy(side, number, relay_number, scan).wait_recv()
        row_copy(
            relay.at[relay_number], side, number, displaced(slab, number), scan, relay_send
        ).start()

    def step(batch, carry):
        for side, relaying in ((0, scan == 0), (1, scan == last)):
            @pl.when(jnp.logical_and(relaying, batch < SLABS // 8))
            def _():
                for one in range(4):
                    pass_on(side, batch * 4 + one)

        for side in range(2):
            @pl.when(present[side])
            def _():
                absorb(side, batch)

        return carry

    def moments_of(first, count):
        at = slice(first, first + count)
        return sum(
            jnp.dot(
                chosen[:, side * SLABS * CAP + first : side * SLABS * CAP + first + count],
                sums[side, at, :].astype(jnp.bfloat16),
                preferred_element_type=jnp.float32,
            )
            for side in range(2)
        )

    settled = 512
    steps = SLABS // BATCH
    lax.fori_loop(0, 3 * steps // 4, step, 0)
    moments = moments_of(0, settled)
    lax.fori_loop(3 * steps // 4, steps, step, 0)

    collect(0)
    smooth = stencil(0, stiffness * velocity)
    moments = moments + moments_of(settled, SLABS * CAP - settled)
    moments = jnp.transpose(moments)
    moments = moments[0:8] + moments[8:16] + moments[16:24]
    m0, m1, m2, m3, m4 = (moments[number : number + 1, :] for number in range(5))

    def coefficients(quarter):
        def one_row(row, at):
            forward = place_scalar[0, row]
            backward = place_scalar[1, row]

            def got(ref):
                return (
                    jnp.where(up, ref[0, forward], 0.0),
                    jnp.where(down, ref[1, backward], 0.0),
                )

            value_f, value_b = got(value)
            slope_f, slope_b = got(slope)
            bend_f, bend_b = got(bend)
            turned[0, at] = value_f + value_b - 2.0 * by_row[row]
            turned[1, at] = slope_f - slope_b
            turned[2, at] = 0.5 * (bend_f + bend_b)

        def eight(step, carry):
            base = pl.multiple_of(quarter * (rows // 4) + step * 8, 8)
            half = (step % 2) * 8
            for one in range(8):
                one_row(base + one, half + one)
            for number in range(3):
                for block in range(blocks):
                    parts_buf[number, pl.ds(base, 8), block * LANES : (block + 1) * LANES] = turned[
                        number, pl.ds(pl.multiple_of(half, 8), 8), block, :
                    ]
            return carry

        lax.fori_loop(0, rows // 32, eight, 0)
        for copy in part_copies(quarter):
            copy.start()

    def part_copies(quarter):
        at = pl.ds(quarter * (rows // 4), rows // 4)
        return [
            pltpu.make_async_copy(parts_buf.at[number, at], ref.at[at], part_sem.at[number, quarter])
            for number, ref in enumerate((part0_ref, part1_ref, part2_ref))
        ]

    def folded(values):
        return sum(values[:, at : at + LANES] for at in range(0, rows, LANES))

    def far_copy(turn, number):
        return pltpu.make_async_remote_copy(
            src_ref=totals.at[turn],
            dst_ref=far_box.at[turn, number],
            send_sem=far_send.at[turn, number],
            recv_sem=far_recv.at[turn, number],
            device_id=far_peer(number),
            device_id_type=MESH,
        )

    for turn in range(ITERS):
        linear = m0 + velocity * (m1 + m2) + 1.5 * velocity * velocity * m3 + (
            0.5 * velocity * velocity * velocity * m4
        )
        curvature = m2 + 2.0 * velocity * m3 + velocity * velocity * m4
        gradient = linear + stiffness * smooth
        direction = gradient / (curvature + 4.0 * stiffness * stiffness)
        scaled = stiffness * direction
        share(
            turn + 1,
            jnp.concatenate(
                [
                    scaled,
                    folded(direction * gradient),
                    folded(curvature * direction * direction + 4.0 * scaled * scaled),
                ],
                axis=1,
            ),
        )
        coefficients(2 * turn)
        collect(turn + 1)
        box = near_box[turn + 1, :, 0, :]
        fields = box[2 : group + 2, :rows]
        beyond = jnp.where(
            jnp.logical_or(above, lax.broadcasted_iota(jnp.int32, (4, rows), 0) < 2),
            box[group : group + 4, :rows], 0.0,
        )
        next1 = jnp.concatenate([box[3 : group + 2, :rows], beyond[2:3]], axis=0)
        next2 = jnp.concatenate([box[4 : group + 2, :rows], beyond[2:4]], axis=0)
        lane_all = lax.broadcasted_iota(jnp.int32, (group, rows), 1)
        right = jnp.where(
            lane_all == rows - 1, pltpu.roll(next1, rows - 1, 1), pltpu.roll(fields, rows - 1, 1)
        )
        cross = jnp.sum(folded(fields * (right + next2)), axis=0, keepdims=True)
        mine = jnp.sum(box[2 : group + 2, rows:], axis=0, keepdims=True)
        mine = mine - jnp.concatenate([jnp.zeros_like(cross), 2.0 * cross], axis=1)
        totals[turn] = mine

        def far_start(number, carry):
            far_copy(turn, number).start()
            return carry

        def far_wait(number, carry):
            far_copy(turn, number).wait_recv()
            return carry

        lax.fori_loop(0, fars - 1, far_start, 0)
        bent = stencil(turn + 1, scaled)
        coefficients(2 * turn + 1)
        lax.fori_loop(0, fars - 1, far_wait, 0)
        mine = mine + jnp.sum(far_box[turn], axis=0)
        upper = jnp.sum(mine[:, :LANES], axis=1, keepdims=True)
        lower = jnp.sum(mine[:, LANES:], axis=1, keepdims=True)
        alpha = upper / lower
        velocity = velocity - alpha * direction
        smooth = smooth - alpha * bent
    out_ref[...] = velocity

    for turn in range(ITERS + 1):
        shares(turn, lambda copy: copy.wait_send())

    def far_left(number, carry):
        for turn in range(ITERS):
            far_copy(turn, number).wait_send()
        return carry

    lax.fori_loop(0, fars - 1, far_left, 0)

    @pl.when(up)
    def _():
        whole_ask(0).wait_send()

    @pl.when(down)
    def _():
        whole_ask(1).wait_send()

    for side, serving in ((0, down), (1, up)):
        @pl.when(serving)
        def _():
            pltpu.make_async_remote_copy(
                src_ref=packed.at[side],
                dst_ref=arrived.at[side],
                send_sem=row_send.at[side],
                recv_sem=row_recv.at[side, 0],
                device_id=(scan, slab),
                device_id_type=MESH,
            ).wait_send()

    @pl.when(edge)
    def _():
        pltpu.make_async_remote_copy(
            src_ref=relay,
            dst_ref=relay,
            send_sem=relay_send,
            recv_sem=relay_recv.at[0],
            device_id=(scan, slab),
            device_id_type=MESH,
        ).wait_send()

    for quarter in range(4):
        for copy in part_copies(quarter):
            copy.wait()


def misfit_kernel(velocity_ref, part0_ref, part1_ref, part2_ref, out_ref, velocity_out_ref):
    rows = out_ref.shape[0]
    across = velocity_ref[...]
    velocity_out_ref[...] = across
    moved = jnp.transpose(jnp.broadcast_to(across, (rows, rows)))
    for at in range(0, out_ref.shape[1], LANES):
        columns = slice(at, at + LANES)
        out_ref[:, columns] = part0_ref[:, columns] + moved * (
            part1_ref[:, columns] + moved * part2_ref[:, columns]
        )


def on_device(volume, velocity0, fetch_slab, fetch_row, modulus_class, modulus_table):
    rows, length = volume.shape[1:]
    blocks = length // LANES
    f32 = jnp.float32
    i32 = jnp.int32
    vmem = pl.BlockSpec(memory_space=pltpu.VMEM)
    smem = pl.BlockSpec(memory_space=pltpu.SMEM)
    anywhere = pl.BlockSpec(memory_space=pl.ANY)
    dma = pltpu.SemaphoreType.DMA
    high, low = filter_parts()
    tile = (blocks, LANES)
    turns = ITERS + 1
    wide = rows + 2 * LANES

    velocity, part0, part1, part2 = pl.pallas_call(
        velocity_kernel,
        name="velocity",
        out_shape=(
            jax.ShapeDtypeStruct((1, rows), f32),
            jax.ShapeDtypeStruct((rows, length), f32),
            jax.ShapeDtypeStruct((rows, length), f32),
            jax.ShapeDtypeStruct((rows, length), f32),
        ),
        in_specs=[smem, vmem, vmem, anywhere, vmem, vmem, vmem, vmem],
        out_specs=(vmem, anywhere, anywhere, anywhere),
        scratch_shapes=[
            pltpu.VMEM((rows, length), f32),
            pltpu.VMEM((rows,) + tile, f32),
            pltpu.VMEM((2, SLABS, 1, LANES), i32),
            pltpu.VMEM((2, SLABS, 1, LANES), i32),
            pltpu.VMEM((2, rows), i32),
            pltpu.VMEM((2, SLABS, 1, LANES), i32),
            pltpu.SMEM((2, SLABS, 1, LANES), i32),
            pltpu.SMEM((2, SLABS, 1, LANES), i32),
            pltpu.SMEM((2, rows), i32),
            pltpu.VMEM((2, SLABS, CAP) + tile, f32),
            pltpu.VMEM((SLABS // 2, CAP) + tile, f32),
            pltpu.VMEM((2, SLABS, CAP) + tile, f32),
            pltpu.VMEM((2, SLABS * CAP) + tile, f32),
            pltpu.VMEM((2, SLABS * CAP) + tile, f32),
            pltpu.VMEM((2, SLABS * CAP) + tile, f32),
            pltpu.VMEM((BATCH * CAP,) + tile, f32),
            pltpu.VMEM((BATCH * CAP,) + tile, f32),
            pltpu.VMEM((BATCH * CAP,) + tile, f32),
            pltpu.VMEM((2, SLABS * CAP, LANES), f32),
            pltpu.VMEM((rows, 2 * SLABS * CAP), jnp.bfloat16),
            pltpu.VMEM((3, rows, length), f32),
            pltpu.VMEM((3, 16) + tile, f32),
            pltpu.VMEM((turns, 12, 1, wide), f32),
            pltpu.VMEM((ITERS, SCANS * LAYERS - 1, 1, 2 * LANES), f32),
            pltpu.VMEM((ITERS, 1, 2 * LANES), f32),
            dma, dma((2,)), dma((2,)), dma((4,)), dma((2,)), dma((2, SLABS)),
            dma((SLABS // 2,)), dma,
            dma((turns, 15)), dma((turns, 12)),
            dma((ITERS, SCANS * LAYERS - 1)), dma((ITERS, SCANS * LAYERS - 1)),
            dma((3, 4)),
        ],
        compiler_params=pltpu.CompilerParams(
            collective_id=0, has_side_effects=True, vmem_limit_bytes=56 * MIB
        ),
    )(
        modulus_table, fetch_slab.reshape(2, rows), fetch_row.reshape(2, rows),
        volume.reshape(rows, length), velocity0, modulus_class, high, low,
    )

    block = 128
    across = pl.BlockSpec((1, block), lambda step: (0, step))
    wide_rows = pl.BlockSpec((block, length), lambda step: (step, 0))
    misfit, velocity = pl.pallas_call(
        misfit_kernel,
        name="misfit",
        grid=(rows // block,),
        out_shape=(
            jax.ShapeDtypeStruct((rows, length), f32),
            jax.ShapeDtypeStruct((1, rows), f32),
        ),
        in_specs=[across, wide_rows, wide_rows, wide_rows],
        out_specs=(wide_rows, across),
    )(velocity, part0, part1, part2)
    return velocity, misfit.reshape(volume.shape)


def solution(mesh):
    return jax.shard_map(
        on_device,
        mesh=mesh,
        in_specs=(
            P("scan", "slab", None),
            P("scan", "slab"),
            P("scan", None, "slab", None),
            P("scan", None, "slab"),
            P("scan", "slab"),
            P(),
        ),
        out_specs=(P("scan", "slab"), P("scan", "slab", None)),
        check_vma=False,
    )
```

```python
import math

import jax
import jax.numpy as jnp
import numpy as np
from jax import lax
from jax.experimental import pallas as pl
from jax.experimental.pallas import tpu as pltpu
from jax.sharding import PartitionSpec as P

BAND = 32
ITERS = 2
CAP = 12
LANES = 128
SCANS = 4
SLABS = 64
LAYERS = 8
BATCH = 2
MESH = pl.DeviceIdType.MESH
MIB = 1024 * 1024

root_three = math.sqrt(3.0)
pole_value = math.sqrt(3.0) - 2.0


def filter_parts():
    source = np.arange(LANES)[:, None]
    column = np.arange(2 * LANES)[None, :]
    lane = column % LANES
    beside = np.where(lane < LANES // 2, lane + LANES, lane - LANES)
    distance = np.abs(source - np.where(column < LANES, lane, beside))
    matrix = np.where(distance <= BAND, root_three * pole_value ** distance, 0.0)
    matrix = matrix.astype(np.float32)
    high = matrix.astype(jnp.bfloat16)
    low = (matrix - high.astype(np.float32)).astype(jnp.bfloat16)
    return jnp.asarray(np.concatenate([high, high])), jnp.asarray(low)


def over(number, by):
    return lax.div(number, jnp.int32(by))


def left_of(number, by):
    return lax.rem(number, jnp.int32(by))


def shifts(number):
    phase = left_of(number, 8)
    wave = over(number, 8)
    half = over(phase + 1, 2)
    shift_z = jnp.where(left_of(phase, 2) == 0, left_of(8 - half, 8), half)
    return shift_z, 2 * left_of(wave, 2) + over(wave, 4), left_of(over(wave, 2), 2)


def displaced(slab, number):
    shift_z, shift_x, shift_c = shifts(number)
    core = left_of(left_of(slab, 2) + shift_c, 2)
    at_x = left_of(over(slab, 2) + shift_x, 4)
    at_z = left_of(over(slab, 8) + shift_z, 8)
    return (at_z * 4 + at_x) * 2 + core


def number_between(source, target):
    shift_c = (target % 2 + 2 - source % 2) % 2
    shift_x = ((target // 2) % 4 + 4 - (source // 2) % 4) % 4
    shift_z = (target // 8 + 8 - source // 8) % 8
    phase = jnp.where(shift_z > 4, 2 * (8 - shift_z), jnp.maximum(2 * shift_z - 1, 0))
    wave = shift_x // 2 + 2 * shift_c + 4 * (shift_x % 2)
    return wave * 8 + phase


def velocity_kernel(
    table_ref, peer_ref, row_ref, volume_ref, velocity_ref, class_ref, high_ref, low_ref,
    out_ref, part0_ref, part1_ref, part2_ref,
    volume, by_row, request, wanting, place, asked, asked_scalar, wanting_scalar, place_scalar,
    packed, relay, arrived, value, slope, bend, middle, beside, own, sums, chosen, parts_buf,
    turned, near_box, far_box, totals,
    volume_sem, ask_send, ask_recv, scalar_sem, row_send, row_recv, relay_recv, relay_send,
    near_send, near_recv, far_send, far_recv, part_sem,
):
    scan = lax.axis_index("scan")
    slab = lax.axis_index("slab")
    rows = velocity_ref.shape[1]
    blocks = volume_ref.shape[1] // LANES
    group = SLABS // LAYERS
    position = slab % group
    layer = slab // group
    fars = SCANS * LAYERS
    last = SCANS - 1
    edge = jnp.logical_or(scan == 0, scan == last)
    down = scan >= 1
    up = scan <= last - 1
    present = (up, down)

    volume_copy = pltpu.make_async_copy(volume_ref, volume, volume_sem)
    volume_copy.start()

    barrier = pltpu.get_barrier_semaphore()

    def near_peer(number):
        return (scan, layer * group + left_of(position + 1 + number, group))

    def far_peer(number):
        other = left_of(scan * LAYERS + layer + 1 + number, fars)
        return (over(other, LAYERS), left_of(other, LAYERS) * group + position)

    below = jnp.logical_and(layer >= 1, position <= 1)
    above = layer <= LAYERS - 2
    to_above = jnp.logical_and(above, position >= group - 2)

    def greet(device):
        pl.semaphore_signal(barrier, inc=1, device_id=device, device_id_type=MESH)

    def greet_rows(number, carry):
        @pl.when(down)
        def _():
            greet((scan - 1, number))

        @pl.when(up)
        def _():
            greet((scan + 1, number))

        return carry

    lax.fori_loop(0, SLABS, greet_rows, 0)
    expected = jnp.where(edge, SLABS, 2 * SLABS)

    earlier = (
        lax.broadcasted_iota(jnp.int32, (rows, rows), 0)
        < lax.broadcasted_iota(jnp.int32, (rows, rows), 1)
    ).astype(jnp.float32).astype(jnp.bfloat16)
    contract = (((1,), (1,)), ((), ()))
    here = lax.broadcasted_iota(jnp.int32, (1, rows), 1)
    for side in range(2):
        peer = peer_ref[side : side + 1, :]
        named = (lax.broadcasted_iota(jnp.int32, (SLABS, rows), 0) == peer).astype(jnp.float32)
        named16 = named.astype(jnp.bfloat16)
        before = jnp.dot(named16, earlier, preferred_element_type=jnp.float32)
        slot = jnp.sum(before * named, axis=0, keepdims=True).astype(jnp.int32)
        at_slot = (lax.broadcasted_iota(jnp.int32, (LANES, rows), 0) == slot).astype(jnp.float32)

        def tabled(numbers):
            high = (at_slot * (numbers // 16).astype(jnp.float32)).astype(jnp.bfloat16)
            low = (at_slot * (numbers % 16).astype(jnp.float32)).astype(jnp.bfloat16)
            table = (
                16.0 * lax.dot_general(named16, high, contract, preferred_element_type=jnp.float32)
                + lax.dot_general(named16, low, contract, preferred_element_type=jnp.float32)
            ).astype(jnp.int32)
            return jnp.clip(table, 0, rows - 1)

        request[side, :, 0, :] = tabled(row_ref[side : side + 1, :])
        wanting[side, :, 0, :] = tabled(here)
        at = number_between(peer, slab) * CAP + jnp.clip(slot, 0, CAP - 1)
        place[side : side + 1, :] = jnp.clip(at, 0, SLABS * CAP - 1)

    volume_copy.wait()

    def relayout(block, carry):
        base = pl.multiple_of(block * 8, 8)
        for part in range(blocks):
            by_row[pl.ds(base, 8), part, :] = volume[
                pl.ds(base, 8), part * LANES : (part + 1) * LANES
            ]
        return carry

    lax.fori_loop(0, rows // 8, relayout, 0)
    pl.semaphore_wait(barrier, expected)

    def ask_copy(side, number):
        return pltpu.make_async_remote_copy(
            src_ref=request.at[side, number],
            dst_ref=asked.at[side, slab],
            send_sem=ask_send.at[side],
            recv_sem=ask_recv.at[side],
            device_id=(scan + 1 - 2 * side, number),
            device_id_type=MESH,
        )

    def ask(number, carry):
        target = left_of(slab + number, SLABS)

        @pl.when(up)
        def _():
            ask_copy(0, target).start()

        @pl.when(down)
        def _():
            ask_copy(1, target).start()

        return carry

    lax.fori_loop(0, SLABS, ask, 0)

    def whole_ask(side):
        return pltpu.make_async_remote_copy(
            src_ref=request.at[side],
            dst_ref=asked.at[side],
            send_sem=ask_send.at[side],
            recv_sem=ask_recv.at[side],
            device_id=(scan, slab),
            device_id_type=MESH,
        )

    def near_copy(turn, index, entry, device):
        return pltpu.make_async_remote_copy(
            src_ref=near_box.at[turn, position + 2],
            dst_ref=near_box.at[turn, entry],
            send_sem=near_send.at[turn, index],
            recv_sem=near_recv.at[turn, entry],
            device_id=device,
            device_id_type=MESH,
        )

    def shares(turn, act):
        for number in range(group - 1):
            act(near_copy(turn, number, position + 2, near_peer(number)))

        @pl.when(below)
        def _():
            for number in range(group):
                act(near_copy(turn, 7 + number, position + group + 2, (scan, (layer - 1) * group + number)))

        @pl.when(to_above)
        def _():
            for number in range(2):
                act(near_copy(turn, 7 + number, position - group + 2, (scan, (layer + 1) * group + number)))

    def share(turn, message):
        near_box[turn, position + 2] = message
        shares(turn, lambda copy: copy.start())

    def collect(turn):
        def wait(entry):
            near_copy(turn, 0, entry, (scan, slab)).wait_recv()

        for entry in range(2, group + 2):
            @pl.when(position + 2 != entry)
            def _():
                wait(entry)

        @pl.when(above)
        def _():
            wait(group + 2)
            wait(group + 3)

        @pl.when(below)
        def _():
            wait(0)
            wait(1)

    lane_row = lax.broadcasted_iota(jnp.int32, (1, rows), 1)

    def stencil(turn, field):
        def entry(offset):
            return near_box[turn, position + 2 + offset, :, :rows]

        lower1 = jnp.where(slab >= 1, entry(-1), 0.0)
        lower2 = jnp.where(slab >= 2, entry(-2), 0.0)
        upper1 = jnp.where(slab <= SLABS - 2, entry(1), 0.0)
        upper2 = jnp.where(slab <= SLABS - 3, entry(2), 0.0)
        left = jnp.where(lane_row == 0, pltpu.roll(lower1, 1, 1), pltpu.roll(field, 1, 1))
        right = jnp.where(
            lane_row == rows - 1, pltpu.roll(upper1, rows - 1, 1), pltpu.roll(field, rows - 1, 1)
        )
        return 4.0 * field - left - right - lower2 - upper2

    weight = jnp.zeros((1, rows), jnp.float32)
    for number in range(4):
        weight = jnp.where(class_ref[...] == number, table_ref[number], weight)
    stiffness = jnp.sqrt(weight)
    velocity = velocity_ref[...]

    wanting_copy = pltpu.make_async_copy(wanting, wanting_scalar, scalar_sem.at[2])
    place_copy = pltpu.make_async_copy(place, place_scalar, scalar_sem.at[3])
    wanting_copy.start()
    place_copy.start()

    def scalar_copy(side):
        return pltpu.make_async_copy(asked.at[side], asked_scalar.at[side], scalar_sem.at[side])

    for side, serving in ((0, down), (1, up)):
        @pl.when(serving)
        def _():
            whole_ask(side).wait_recv()
            scalar_copy(side).start()

    for side, serving in ((0, down), (1, up)):
        @pl.when(serving)
        def _():
            scalar_copy(side).wait()

    def row_copy(source, side, number, target, target_scan, send_sem):
        return pltpu.make_async_remote_copy(
            src_ref=source,
            dst_ref=arrived.at[side, number],
            send_sem=send_sem,
            recv_sem=row_recv.at[side, number],
            device_id=(target_scan, target),
            device_id_type=MESH,
        )

    def relay_copy(side, number, relay_number, target_scan):
        return pltpu.make_async_remote_copy(
            src_ref=packed.at[side, number],
            dst_ref=relay.at[relay_number],
            send_sem=row_send.at[side],
            recv_sem=relay_recv.at[relay_number],
            device_id=(target_scan, slab),
            device_id_type=MESH,
        )

    def serve(side, number, target, relayed_scan):
        target_scan = scan - 1 + 2 * side
        relay_number = (number // 16) * 8 + number % 8
        relayed = jnp.logical_and(scan == relayed_scan, (number // 8) % 2 == 1)
        for slot in range(CAP):
            packed[side, number, slot] = by_row[asked_scalar[side, target, 0, slot]]

        @pl.when(relayed)
        def _():
            relay_copy(side, number, relay_number, target_scan).start()

        @pl.when(jnp.logical_not(relayed))
        def _():
            row_copy(
                packed.at[side, number], side, number, target, target_scan, row_send.at[side]
            ).start()

    def send(number, carry):
        target = displaced(slab, number)

        @pl.when(down)
        def _():
            serve(0, number, target, 1)

        @pl.when(up)
        def _():
            serve(1, number, target, 2)

        return carry

    lax.fori_loop(0, SLABS, send, 0)
    blank = jnp.zeros((1, 2 * LANES), jnp.float32)
    share(0, jnp.concatenate([stiffness * velocity, blank], axis=1))

    wanting_copy.wait()
    place_copy.wait()
    for side in range(2):
        across = place[side : side + 1, :].astype(jnp.float32)
        upright = jnp.transpose(jnp.broadcast_to(across, (LANES, rows)))
        lane = lax.broadcasted_iota(jnp.int32, (rows, LANES), 1).astype(jnp.float32)
        for block in range(SLABS * CAP // LANES):
            at = side * SLABS * CAP + block * LANES
            chosen[:, at : at + LANES] = (
                (upright == lane + float(block * LANES)).astype(jnp.float32).astype(jnp.bfloat16)
            )

        @pl.when(jnp.logical_not(present[side]))
        def _():
            sums[side] = jnp.zeros(sums.shape[1:], jnp.float32)

    lane8 = lax.broadcasted_iota(jnp.int32, (8, LANES), 1)
    zero8 = jnp.zeros((8, LANES), jnp.float32)
    batch_rows = BATCH * CAP

    def absorb(side, batch):
        for one in range(BATCH):
            number = batch * BATCH + one
            row_copy(packed.at[side, number], side, number, slab, scan, row_send.at[side]).wait_recv()
        voxels = arrived[side, pl.ds(batch * BATCH, BATCH)].reshape(batch_rows * blocks, LANES)
        top = voxels.astype(jnp.bfloat16)
        rest = (voxels - top.astype(jnp.float32)).astype(jnp.bfloat16)
        both = jnp.dot(
            jnp.concatenate([top, rest], axis=1), high_ref[...], preferred_element_type=jnp.float32
        ) + jnp.dot(top, low_ref[...], preferred_element_type=jnp.float32)
        middle[...] = both[:, :LANES].reshape(batch_rows, blocks, LANES)
        beside[...] = both[:, LANES:].reshape(batch_rows, blocks, LANES)
        for chunk in range(BATCH):
            source = displaced_back(batch * BATCH + chunk)
            for slot in range(CAP):
                own[chunk * CAP + slot] = by_row[wanting_scalar[side, source, 0, slot]]

        def combine(eight, carry):
            at = pl.ds(pl.multiple_of(eight * 8, 8), 8)
            to = pl.ds(pl.multiple_of(batch * batch_rows + eight * 8, 8), 8)
            coeffs = []
            for block in range(blocks):
                left = beside[at, block - 1, :] if block > 0 else zero8
                right = beside[at, block + 1, :] if block < blocks - 1 else zero8
                coeffs.append(middle[at, block, :] + jnp.where(lane8 < LANES // 2, left, right))
            to_right = [pltpu.roll(one, 1, 1) for one in coeffs]
            to_left = [pltpu.roll(one, LANES - 1, 1) for one in coeffs]
            total = [zero8] * 5
            for block in range(blocks):
                prior = jnp.where(lane8 == 0, to_right[block - 1] if block > 0 else zero8, to_right[block])
                after = jnp.where(
                    lane8 == LANES - 1,
                    to_left[block + 1] if block < blocks - 1 else zero8,
                    to_left[block],
                )
                ends = prior + after
                v = (ends + 4.0 * coeffs[block]) * (1.0 / 6.0)
                s = 0.5 * (after - prior)
                b = ends - 2.0 * coeffs[block]
                off = v - own[at, block, :]
                value[side, to, block, :] = v
                slope[side, to, block, :] = s
                bend[side, to, block, :] = b
                total[0] += s * off
                total[1] += b * off
                total[2] += s * s
                total[3] += s * b
                total[4] += b * b
            column = zero8
            for number in range(5):
                summed = jnp.sum(total[number], axis=1, keepdims=True)
                if side == 1 and number in (0, 3):
                    summed = -summed
                column = jnp.where(lane8 % 8 == number, summed, column)
            first = column.astype(jnp.bfloat16).astype(jnp.float32)
            second = (column - first).astype(jnp.bfloat16).astype(jnp.float32)
            third = (column - first - second).astype(jnp.bfloat16).astype(jnp.float32)
            column = jnp.where(lane8 < 8, first, jnp.where(lane8 < 16, second, third))
            sums[side, to, :] = jnp.where(lane8 < 24, column, 0.0)
            return carry

        lax.fori_loop(0, batch_rows // 8, combine, 0)

    def displaced_back(number):
        shift_z, shift_x, shift_c = shifts(number)
        core = left_of(left_of(slab, 2) + 2 - shift_c, 2)
        at_x = left_of(over(slab, 2) + 4 - shift_x, 4)
        at_z = left_of(over(slab, 8) + 8 - shift_z, 8)
        return (at_z * 4 + at_x) * 2 + core

    def pass_on(side, relay_number):
        number = (relay_number // 8) * 16 + 8 + relay_number % 8
        relay_copy(side, number, relay_number, scan).wait_recv()
        row_copy(
            relay.at[relay_number], side, number, displaced(slab, number), scan, relay_send
        ).start()

    def step(batch, carry):
        for side, relaying in ((0, scan == 0), (1, scan == last)):
            @pl.when(jnp.logical_and(relaying, batch < SLABS // 8))
            def _():
                for one in range(4):
                    pass_on(side, batch * 4 + one)

        for side in range(2):
            @pl.when(present[side])
            def _():
                absorb(side, batch)

        return carry

    def moments_of(first, count):
        at = slice(first, first + count)
        return sum(
            jnp.dot(
                chosen[:, side * SLABS * CAP + first : side * SLABS * CAP + first + count],
                sums[side, at, :].astype(jnp.bfloat16),
                preferred_element_type=jnp.float32,
            )
            for side in range(2)
        )

    settled = 512
    steps = SLABS // BATCH
    lax.fori_loop(0, 3 * steps // 4, step, 0)
    moments = moments_of(0, settled)
    lax.fori_loop(3 * steps // 4, steps, step, 0)

    collect(0)
    smooth = stencil(0, stiffness * velocity)
    moments = moments + moments_of(settled, SLABS * CAP - settled)
    moments = jnp.transpose(moments)
    moments = moments[0:8] + moments[8:16] + moments[16:24]
    m0, m1, m2, m3, m4 = (moments[number : number + 1, :] for number in range(5))

    def coefficients(quarter):
        def one_row(row, at):
            forward = place_scalar[0, row]
            backward = place_scalar[1, row]

            def got(ref):
                return (
                    jnp.where(up, ref[0, forward], 0.0),
                    jnp.where(down, ref[1, backward], 0.0),
                )

            value_f, value_b = got(value)
            slope_f, slope_b = got(slope)
            bend_f, bend_b = got(bend)
            turned[0, at] = value_f + value_b - 2.0 * by_row[row]
            turned[1, at] = slope_f - slope_b
            turned[2, at] = 0.5 * (bend_f + bend_b)

        def eight(step, carry):
            base = pl.multiple_of(quarter * (rows // 4) + step * 8, 8)
            half = (step % 2) * 8
            for one in range(8):
                one_row(base + one, half + one)
            for number in range(3):
                for block in range(blocks):
                    parts_buf[number, pl.ds(base, 8), block * LANES : (block + 1) * LANES] = turned[
                        number, pl.ds(pl.multiple_of(half, 8), 8), block, :
                    ]
            return carry

        lax.fori_loop(0, rows // 32, eight, 0)
        for copy in part_copies(quarter):
            copy.start()

    def part_copies(quarter):
        at = pl.ds(quarter * (rows // 4), rows // 4)
        return [
            pltpu.make_async_copy(parts_buf.at[number, at], ref.at[at], part_sem.at[number, quarter])
            for number, ref in enumerate((part0_ref, part1_ref, part2_ref))
        ]

    def folded(values):
        return sum(values[:, at : at + LANES] for at in range(0, rows, LANES))

    def far_copy(turn, number):
        return pltpu.make_async_remote_copy(
            src_ref=totals.at[turn],
            dst_ref=far_box.at[turn, number],
            send_sem=far_send.at[turn, number],
            recv_sem=far_recv.at[turn, number],
            device_id=far_peer(number),
            device_id_type=MESH,
        )

    def rows_left():
        @pl.when(up)
        def _():
            whole_ask(0).wait_send()

        @pl.when(down)
        def _():
            whole_ask(1).wait_send()

        for side, serving in ((0, down), (1, up)):
            @pl.when(serving)
            def _():
                pltpu.make_async_remote_copy(
                    src_ref=packed.at[side],
                    dst_ref=arrived.at[side],
                    send_sem=row_send.at[side],
                    recv_sem=row_recv.at[side, 0],
                    device_id=(scan, slab),
                    device_id_type=MESH,
                ).wait_send()

        @pl.when(edge)
        def _():
            pltpu.make_async_remote_copy(
                src_ref=relay,
                dst_ref=relay,
                send_sem=relay_send,
                recv_sem=relay_recv.at[0],
                device_id=(scan, slab),
                device_id_type=MESH,
            ).wait_send()

    def far_left(turn):
        def one(number, carry):
            far_copy(turn, number).wait_send()
            return carry

        lax.fori_loop(0, fars - 1, one, 0)

    for turn in range(ITERS):
        linear = m0 + velocity * (m1 + m2) + 1.5 * velocity * velocity * m3 + (
            0.5 * velocity * velocity * velocity * m4
        )
        curvature = m2 + 2.0 * velocity * m3 + velocity * velocity * m4
        gradient = linear + stiffness * smooth
        direction = gradient / (curvature + 4.0 * stiffness * stiffness)
        scaled = stiffness * direction
        share(
            turn + 1,
            jnp.concatenate(
                [
                    scaled,
                    folded(direction * gradient),
                    folded(curvature * direction * direction + 4.0 * scaled * scaled),
                ],
                axis=1,
            ),
        )
        coefficients(2 * turn)
        collect(turn + 1)
        box = near_box[turn + 1, :, 0, :]
        fields = box[2 : group + 2, :rows]
        beyond = jnp.where(
            jnp.logical_or(above, lax.broadcasted_iota(jnp.int32, (4, rows), 0) < 2),
            box[group : group + 4, :rows], 0.0,
        )
        next1 = jnp.concatenate([box[3 : group + 2, :rows], beyond[2:3]], axis=0)
        next2 = jnp.concatenate([box[4 : group + 2, :rows], beyond[2:4]], axis=0)
        lane_all = lax.broadcasted_iota(jnp.int32, (group, rows), 1)
        right = jnp.where(
            lane_all == rows - 1, pltpu.roll(next1, rows - 1, 1), pltpu.roll(fields, rows - 1, 1)
        )
        cross = jnp.sum(folded(fields * (right + next2)), axis=0, keepdims=True)
        mine = jnp.sum(box[2 : group + 2, rows:], axis=0, keepdims=True)
        mine = mine - jnp.concatenate([jnp.zeros_like(cross), 2.0 * cross], axis=1)
        totals[turn] = mine

        def far_start(number, carry):
            far_copy(turn, number).start()
            return carry

        def far_wait(number, carry):
            far_copy(turn, number).wait_recv()
            return carry

        lax.fori_loop(0, fars - 1, far_start, 0)
        bent = stencil(turn + 1, scaled)
        coefficients(2 * turn + 1)
        shares(turn + 1, lambda copy: copy.wait_send())
        if turn == 0:
            rows_left()
            shares(0, lambda copy: copy.wait_send())
        else:
            far_left(turn - 1)
        lax.fori_loop(0, fars - 1, far_wait, 0)
        mine = mine + jnp.sum(far_box[turn], axis=0)
        upper = jnp.sum(mine[:, :LANES], axis=1, keepdims=True)
        lower = jnp.sum(mine[:, LANES:], axis=1, keepdims=True)
        alpha = upper / lower
        velocity = velocity - alpha * direction
        smooth = smooth - alpha * bent
    out_ref[...] = velocity

    far_left(ITERS - 1)
    for quarter in range(4):
        for copy in part_copies(quarter):
            copy.wait()


def misfit_kernel(velocity_ref, part0_ref, part1_ref, part2_ref, out_ref, velocity_out_ref):
    rows = out_ref.shape[0]
    across = velocity_ref[...]
    velocity_out_ref[...] = across
    moved = jnp.transpose(jnp.broadcast_to(across, (rows, rows)))
    for at in range(0, out_ref.shape[1], LANES):
        columns = slice(at, at + LANES)
        out_ref[:, columns] = part0_ref[:, columns] + moved * (
            part1_ref[:, columns] + moved * part2_ref[:, columns]
        )


def on_device(volume, velocity0, fetch_slab, fetch_row, modulus_class, modulus_table):
    rows, length = volume.shape[1:]
    blocks = length // LANES
    f32 = jnp.float32
    i32 = jnp.int32
    vmem = pl.BlockSpec(memory_space=pltpu.VMEM)
    smem = pl.BlockSpec(memory_space=pltpu.SMEM)
    anywhere = pl.BlockSpec(memory_space=pl.ANY)
    dma = pltpu.SemaphoreType.DMA
    high, low = filter_parts()
    tile = (blocks, LANES)
    turns = ITERS + 1
    wide = rows + 2 * LANES

    velocity, part0, part1, part2 = pl.pallas_call(
        velocity_kernel,
        name="velocity",
        out_shape=(
            jax.ShapeDtypeStruct((1, rows), f32),
            jax.ShapeDtypeStruct((rows, length), f32),
            jax.ShapeDtypeStruct((rows, length), f32),
            jax.ShapeDtypeStruct((rows, length), f32),
        ),
        in_specs=[smem, vmem, vmem, anywhere, vmem, vmem, vmem, vmem],
        out_specs=(vmem, anywhere, anywhere, anywhere),
        scratch_shapes=[
            pltpu.VMEM((rows, length), f32),
            pltpu.VMEM((rows,) + tile, f32),
            pltpu.VMEM((2, SLABS, 1, LANES), i32),
            pltpu.VMEM((2, SLABS, 1, LANES), i32),
            pltpu.VMEM((2, rows), i32),
            pltpu.VMEM((2, SLABS, 1, LANES), i32),
            pltpu.SMEM((2, SLABS, 1, LANES), i32),
            pltpu.SMEM((2, SLABS, 1, LANES), i32),
            pltpu.SMEM((2, rows), i32),
            pltpu.VMEM((2, SLABS, CAP) + tile, f32),
            pltpu.VMEM((SLABS // 2, CAP) + tile, f32),
            pltpu.VMEM((2, SLABS, CAP) + tile, f32),
            pltpu.VMEM((2, SLABS * CAP) + tile, f32),
            pltpu.VMEM((2, SLABS * CAP) + tile, f32),
            pltpu.VMEM((2, SLABS * CAP) + tile, f32),
            pltpu.VMEM((BATCH * CAP,) + tile, f32),
            pltpu.VMEM((BATCH * CAP,) + tile, f32),
            pltpu.VMEM((BATCH * CAP,) + tile, f32),
            pltpu.VMEM((2, SLABS * CAP, LANES), f32),
            pltpu.VMEM((rows, 2 * SLABS * CAP), jnp.bfloat16),
            pltpu.VMEM((3, rows, length), f32),
            pltpu.VMEM((3, 16) + tile, f32),
            pltpu.VMEM((turns, 12, 1, wide), f32),
            pltpu.VMEM((ITERS, SCANS * LAYERS - 1, 1, 2 * LANES), f32),
            pltpu.VMEM((ITERS, 1, 2 * LANES), f32),
            dma, dma((2,)), dma((2,)), dma((4,)), dma((2,)), dma((2, SLABS)),
            dma((SLABS // 2,)), dma,
            dma((turns, 15)), dma((turns, 12)),
            dma((ITERS, SCANS * LAYERS - 1)), dma((ITERS, SCANS * LAYERS - 1)),
            dma((3, 4)),
        ],
        compiler_params=pltpu.CompilerParams(
            collective_id=0, has_side_effects=True, vmem_limit_bytes=56 * MIB
        ),
    )(
        modulus_table, fetch_slab.reshape(2, rows), fetch_row.reshape(2, rows),
        volume.reshape(rows, length), velocity0, modulus_class, high, low,
    )

    block = 128
    across = pl.BlockSpec((1, block), lambda step: (0, step))
    wide_rows = pl.BlockSpec((block, length), lambda step: (step, 0))
    misfit, velocity = pl.pallas_call(
        misfit_kernel,
        name="misfit",
        grid=(rows // block,),
        out_shape=(
            jax.ShapeDtypeStruct((rows, length), f32),
            jax.ShapeDtypeStruct((1, rows), f32),
        ),
        in_specs=[across, wide_rows, wide_rows, wide_rows],
        out_specs=(wide_rows, across),
    )(velocity, part0, part1, part2)
    return velocity, misfit.reshape(volume.shape)


def solution(mesh):
    return jax.shard_map(
        on_device,
        mesh=mesh,
        in_specs=(
            P("scan", "slab", None),
            P("scan", "slab"),
            P("scan", None, "slab", None),
            P("scan", None, "slab"),
            P("scan", "slab"),
            P(),
        ),
        out_specs=(P("scan", "slab"), P("scan", "slab", None)),
        check_vma=False,
    )
```
